1024 devices in a mesh: group: 8 (over y, core), dx: 16 (over z_hi, x), dy: 8 (over z_lo).
Axes of the slice: x: 4, y: 4, z: 32 (z_hi: 4, z_lo: 8; z = z_hi * 8 + z_lo), core: 2. Of those that a mesh axis runs over, the one named last changes fastest.
Arguments:
- tracers: float32 [64, 32, 128, 1024], P('group', None, 'dx', 'dy'), may hold values from -4 to 4
- reaction: float32 [64, 8], P('group'), may hold values from -0.2 to 0.2
- velocity: float32 [3, 32, 128, 1024], P(None, 'group', 'dx', 'dy'), may hold values from -6 to 6
- thickness: float32 [32, 128, 1024], P('group', 'dx', 'dy'), may hold values from 0.4 to 1
- sea_mask: int32 [128, 1024], P('dx', 'dy'), may hold values 0 or 1
- bottom: int32 [128, 1024], P('dx', 'dy'), may hold values from 1 to 32
- diffusivity: float32 [32, 128, 1024], P(None, 'dx', 'dy'), may hold values from 0.05 to 5
Outputs:
- tracers_out: float32 [64, 32, 128, 1024], P('group', None, 'dx', 'dy')
The draws below stay inside these ranges and needn't reach their ends.
All inputs are finite; a program needn't handle non-finite values. No bound on the sum of `sea_mask` on one device may be relied on, other than what follows from the above.
Results may differ from the reference program's by a relative error of at most 0.0003.
Values sent between devices are 32-bit elements; how exact they have to be, the bound alone decides.
No kernel may reach another device: no remote copies, remote signals or barrier semaphores. Data moves between devices by JAX's collectives and lax.ppermute only.
A program may use at most 64 MiB of HBM per device.

```python
import math
import jax
import jax.numpy as jnp
from jax import lax

NZ = 32
TR = 8
TSTEPS = 2
NX = 128
NY = 1024
NTR = 64
N_GROUP = 8


def set_ends(values, rng, least, top_value):
    shape = values.shape
    index_at = [jax.random.randint(jax.random.fold_in(rng, axis), (), 0, shape[axis]) for axis in range(len(shape))]
    values = values.at[tuple(index_at)].set(least)
    longest = shape.index(max(shape))
    index_at[longest] = (index_at[longest] + 1) % shape[longest]
    return values.at[tuple(index_at)].set(top_value)


def shard_levels(rng, dims, shards, low, high):
    level = 1.0
    for dim, shards_of in shards:
        draws = jax.random.uniform(jax.random.fold_in(jax.random.fold_in(rng, 6), dim), (shards_of,), jnp.float32, low / len(shards), high / len(shards))
        level = level * jnp.repeat(jnp.exp(draws), dims[dim] // shards_of).reshape((-1,) + (1,) * (len(dims) - 1 - dim))
    return level


def gaussian(key, dims, scale, limit, pieces=(), kind=jnp.bfloat16):
    factor_of = shard_levels(key, dims, pieces, -0.22, 0.18) if pieces else 1.0
    values = jax.random.normal(key, dims, jnp.float32) * scale * factor_of
    return jnp.minimum(jnp.maximum(values, -limit), limit).astype(kind)


def setup_inputs(seed: int = 0) -> dict:
    key_of = jax.random.split(jax.random.key(seed), 8)
    return {
        "tracers": gaussian(key_of[0], (NTR, NZ, NX, NY), 1.0, 4.0, ((0, 8), (2, 16), (3, 8)), jnp.float32),
        "reaction": gaussian(key_of[1], (NTR, TR), 0.05, 0.2, ((0, 8),), jnp.float32),
        "velocity": gaussian(key_of[2], (3, NZ, NX, NY), 1.0, 6.0, ((1, 8), (2, 16), (3, 8)), jnp.float32),
        "thickness": jnp.clip(0.4 + 0.6 * jax.random.uniform(key_of[3], (NZ, NX, NY), jnp.float32) ** shard_levels(key_of[3], (NZ, NX, NY), ((0, 8), (1, 16), (2, 8)), -0.2, 0.2), 0.4, 1.0),
        "sea_mask": set_ends((jax.random.randint(key_of[4], (NX, NY), 0, 10) < 9).astype(jnp.int32), jax.random.fold_in(key_of[4], 1), 0, 1),
        "bottom": set_ends(jax.random.randint(key_of[5], (NX, NY), 1, NZ + 1), jax.random.fold_in(key_of[5], 1), 1, NZ).astype(jnp.int32),
        "diffusivity": jnp.clip(jnp.exp(math.log(5.0) - 4.6051702 * jax.random.uniform(key_of[6], (NZ, NX, NY), jnp.float32) ** shard_levels(key_of[6], (NZ, NX, NY), ((1, 16), (2, 8)), -0.2, 0.2)), 0.05, 5.0),
    }


def take_run(values, offset, length, along_dim):
    return lax.slice_in_dim(values, offset, offset + length, axis=values.ndim + along_dim)


def face_fluxes(padded, courant, along_dim, length):
    outer_lo = take_run(padded, 0, length + 3, along_dim)
    inner_lo = take_run(padded, 1, length + 3, along_dim)
    inner_hi = take_run(padded, 2, length + 3, along_dim)
    outer_hi = take_run(padded, 3, length + 3, along_dim)
    edge_vals = (7.0 / 12.0) * (inner_lo + inner_hi) - (1.0 / 12.0) * (outer_lo + outer_hi)
    edge_vals = jnp.minimum(jnp.maximum(edge_vals, jnp.minimum(inner_lo, inner_hi)), jnp.maximum(inner_lo, inner_hi))
    centre = take_run(padded, 2, length + 2, along_dim)
    left_edge = take_run(edge_vals, 0, length + 2, along_dim)
    right_edge = take_run(edge_vals, 1, length + 2, along_dim)
    slopes = right_edge - left_edge
    curves = 6.0 * centre - 3.0 * (left_edge + right_edge)
    right_west = take_run(right_edge, 0, length + 1, along_dim)
    slope_west = take_run(slopes, 0, length + 1, along_dim)
    curve_west = take_run(curves, 0, length + 1, along_dim)
    left_east = take_run(left_edge, 1, length + 1, along_dim)
    slope_east = take_run(slopes, 1, length + 1, along_dim)
    curve_east = take_run(curves, 1, length + 1, along_dim)
    upwind = right_west - 0.5 * courant * (slope_west - (1.0 - courant * (2.0 / 3.0)) * curve_west)
    reverse = -courant
    downwind = left_east + 0.5 * reverse * (slope_east + (1.0 - reverse * (2.0 / 3.0)) * curve_east)
    return courant * jnp.where(courant > 0, upwind, downwind)


def advect(padded, flux_pad, wet_pad):
    count_x = padded.shape[-2] - 6
    count_y = padded.shape[-1] - 6
    wet_cells = wet_pad[:, 1:-1, 1:-1]
    courant_x = flux_pad[0][:, 0:count_x + 1, 1:-1] * wet_pad[:, 0:count_x + 1, 1:-1] * wet_pad[:, 1:count_x + 2, 1:-1]
    flux_x = face_fluxes(padded[..., 3:-3], courant_x, -2, count_x)
    courant_y = flux_pad[1][:, 1:-1, 0:count_y + 1] * wet_pad[:, 1:-1, 0:count_y + 1] * wet_pad[:, 1:-1, 1:count_y + 2]
    flux_y = face_fluxes(padded[..., 3:-3, :], courant_y, -1, count_y)
    centre = padded[..., 3:-3, 3:-3]
    wet_below = jnp.concatenate([wet_cells[1:], jnp.zeros_like(wet_cells[:1])], axis=0)
    courant_z = flux_pad[2][:, 1:-1, 1:-1] * wet_cells * wet_below
    cells_below = jnp.concatenate([centre[..., 1:, :, :], jnp.zeros_like(centre[..., :1, :, :])], axis=-3)
    flux_z = courant_z * jnp.where(courant_z > 0, centre, cells_below)
    flux_above = jnp.concatenate([jnp.zeros_like(flux_z[..., :1, :, :]), flux_z[..., :-1, :, :]], axis=-3)
    return centre - ((flux_x[..., 1:, :] - flux_x[..., :-1, :]) + (flux_y[..., 1:] - flux_y[..., :-1]) + (flux_z - flux_above))


def mixing_factors(diffusivity, wet_cells):
    wet_below = jnp.concatenate([wet_cells[1:], jnp.zeros_like(wet_cells[:1])], axis=0)
    coupling = diffusivity * wet_cells * wet_below
    inverses = []
    ratios = []
    lowers = []
    for level_idx in range(coupling.shape[0]):
        upper_c = coupling[level_idx]
        if level_idx > 0:
            lower_c = coupling[level_idx - 1]
            diagonal = 1.0 + lower_c + upper_c + lower_c * ratios[-1]
        else:
            lower_c = jnp.zeros_like(upper_c)
            diagonal = 1.0 + upper_c
        inverse = 1.0 / diagonal
        inverses.append(inverse)
        ratios.append(-upper_c * inverse)
        lowers.append(lower_c)
    return inverses, ratios, lowers


def solve(right_side, factors):
    inverses, ratios, lowers = factors
    forward = []
    for level_idx in range(len(inverses)):
        if level_idx > 0:
            forward.append((right_side[..., level_idx, :, :] + lowers[level_idx] * forward[-1]) * inverses[level_idx])
        else:
            forward.append(right_side[..., 0, :, :] * inverses[0])
    result = [forward[-1]]
    for level_idx in range(len(inverses) - 2, -1, -1):
        result.append(forward[level_idx] - ratios[level_idx] * result[-1])
    return jnp.stack(result[::-1], axis=-3)


def react(group_tracers, group_rates):
    return group_tracers + group_tracers * jnp.einsum("ab,bzxy->azxy", group_rates, group_tracers, precision=lax.Precision.HIGHEST)


def reference(tracers, reaction, velocity, thickness, sea_mask, bottom, diffusivity):
    fluxes = 0.3 * jnp.tanh(velocity) * thickness[None]
    depth_cells = (sea_mask * bottom).astype(jnp.float32)
    flux_pad = jnp.pad(fluxes, ((0, 0), (0, 0), (1, 1), (1, 1)))
    depth_pad = jnp.pad(depth_cells, 1)
    levels = jnp.arange(NZ).astype(jnp.float32)
    wet_pad = (levels[:, None, None] < depth_pad[None]).astype(jnp.float32)
    wet_cells = wet_pad[:, 1:-1, 1:-1]
    factors = mixing_factors(diffusivity, wet_cells)
    grouped = (tracers * wet_cells[None]).reshape(N_GROUP, TR, NZ, NX, NY)
    group_rates = reaction.reshape(N_GROUP, TR, TR)

    def transport(single):
        padded = jnp.pad(single, ((0, 0), (3, 3), (3, 3)))
        return solve(advect(padded, flux_pad, wet_pad), factors)

    def one_group(members):
        reacted = react(members[0], members[1])
        return lax.map(transport, reacted)

    for time_step in range(TSTEPS):
        grouped = lax.map(one_group, (grouped, group_rates))
    return grouped.reshape(NTR, NZ, NX, NY)
```

```python
import functools

import jax
import jax.numpy as jnp
from jax import lax
from jax.experimental import pallas as pl
from jax.experimental.pallas import tpu as pltpu
from jax.sharding import PartitionSpec as P

INTERPRET = False
XS = 4
NZ = 32
TR = 8
LANES = 128
HALO = 6
PIECES = {"O": (0, 8), "A": (8, 8), "B": (16, 8), "C": (24, 8)}


def spot(row):
    if row < 0:
        return 12 + row
    return row if row < 8 else row + 4


def vmem(count):
    return [pl.BlockSpec(memory_space=pltpu.VMEM)] * count


def shape_of(*dims):
    return jax.ShapeDtypeStruct(dims, jnp.float32)


def call(body, outs, scalars, arrays, scratch=()):
    return pl.pallas_call(
        body,
        out_shape=outs,
        in_specs=[pl.BlockSpec(memory_space=pltpu.SMEM)] * len(scalars) + vmem(len(arrays)),
        out_specs=vmem(len(outs)),
        scratch_shapes=list(scratch),
        interpret=INTERPRET,
    )(*scalars, *arrays)


def spun(rates_ref):
    rates = rates_ref[...]
    tracer = lax.broadcasted_iota(jnp.int32, (TR, TR), 0)
    other = lax.broadcasted_iota(jnp.int32, (TR, TR), 1)
    spins = []
    for shift in range(TR):
        picked = jnp.where(other == (tracer + TR - shift) % TR, rates, 0.0)
        spins.append(jnp.broadcast_to(jnp.sum(picked, axis=1, keepdims=True), (TR, LANES)))
    return spins


def react(value, rates):
    total = rates[0] * value
    for shift in range(1, TR):
        total = total + rates[shift] * pltpu.roll(value, shift, 0)
    return value + value * total


def first_kernel(x_ref, tracers_ref, sea_ref, bottom_ref, rates_ref, hi_ref, lo_ref, *far_refs):
    depth = sea_ref[...] * bottom_ref[...]
    depths = [jnp.broadcast_to(depth[row : row + 1], (TR, LANES)) for row in range(8)]
    rates = spun(rates_ref)

    def level(k, carry):
        for row in range(8):
            value = tracers_ref[pl.ds(k * 8 + row, TR, stride=NZ * 8), :]
            value = react(jnp.where(k < depths[row], value, 0.0), rates)
            if row < HALO:
                lo_ref[k, row] = value
            if row >= 8 - HALO:
                hi_ref[k, row - (8 - HALO)] = value
        return carry

    lax.fori_loop(0, NZ, level, 0)
    for far_ref, (first, count) in zip(far_refs, PIECES.values()):

        @pl.when(x_ref[0] == XS - 1)
        def _():
            far_ref[...] = hi_ref[first : first + count]

        @pl.when(x_ref[0] != XS - 1)
        def _():
            far_ref[...] = lo_ref[first : first + count]


def pack(values, rows):
    lane = lax.broadcasted_iota(jnp.int32, (TR, LANES), 1)
    slot = lane // 8
    east = west = jnp.zeros((TR, LANES), jnp.float32)
    for value, row in zip(values, rows):
        place = 8 * (row + 3)
        here = slot == row + 3
        east = jnp.where(here, pltpu.roll(value, (place + 3) % LANES, 1), east)
        west = jnp.where(here, pltpu.roll(value, (place + 5) % LANES, 1), west)
    return east, west


def join_kernel(x_ref, hi_ref, lo_ref, west_ref, east_ref, *refs):
    pieces, (all_ref, pack_east_ref, pack_west_ref) = refs[:4], refs[4:]
    for near_ref, owner, base in ((west_ref, 0, 0), (east_ref, XS - 1, HALO + 8)):

        @pl.when(x_ref[0] == owner)
        def _():
            for piece_ref, (first, count) in zip(pieces, PIECES.values()):
                all_ref[first : first + count, base : base + HALO] = piece_ref[...]

        @pl.when(x_ref[0] != owner)
        def _():
            all_ref[:, base : base + HALO] = near_ref[...]

    all_ref[:, HALO : 2 * HALO] = lo_ref[...]
    all_ref[:, 2 * HALO : 2 * HALO + 2] = hi_ref[:, HALO - 2 : HALO]
    rows = list(range(-3, 11))

    def level(k, carry):
        packed = pack([all_ref[k, row + HALO] for row in rows], rows)
        pack_east_ref[k], pack_west_ref[k] = packed
        return carry

    lax.fori_loop(0, NZ, level, 0)


UX, AX, BX, UY, AY, BY, CZ, INV, RATIO, LOWER = range(0, 160, 16)


def coefficient_kernel(gathered_ref, out_ref):
    def level(k, carry):
        ratio_before, lower = carry
        for source, at in ((0, UX), (16, UY)):
            courant = gathered_ref[k, source : source + 16]
            size = jnp.abs(courant)
            out_ref[k, at : at + 16] = courant
            out_ref[k, at + 16 : at + 32] = 0.5 * size
            out_ref[k, at + 32 : at + 48] = 1.0 - size * (2.0 / 3.0)
        out_ref[k, CZ : CZ + 16] = gathered_ref[k, 32:48]
        upper = gathered_ref[k, 48:64]
        inverse = 1.0 / (1.0 + lower + upper + lower * ratio_before)
        ratio = -upper * inverse
        out_ref[k, INV : INV + 16] = inverse
        out_ref[k, RATIO : RATIO + 16] = ratio
        out_ref[k, LOWER : LOWER + 16] = lower
        return ratio, upper

    zero = jnp.zeros((16, LANES), jnp.float32)
    lax.fori_loop(0, NZ, level, (zero, zero))


def edge(outer_lo, inner_lo, inner_hi, outer_hi):
    value = 7.0 / 12.0 * (inner_lo + inner_hi) - 1.0 / 12.0 * (outer_lo + outer_hi)
    return jnp.minimum(
        jnp.maximum(value, jnp.minimum(inner_lo, inner_hi)), jnp.maximum(inner_lo, inner_hi)
    )


def face(courant, half, slope, low_edge, near, high_edge, low_cell, high_cell):
    positive = courant > 0
    far = jnp.where(positive, low_edge, high_edge)
    cell = jnp.where(positive, low_cell, high_cell)
    curve = 6.0 * cell - 3.0 * (near + far)
    return courant * (near - half * ((near - far) - slope * curve))


def ahead(value, count):
    return pltpu.roll(value, (LANES - count) % LANES, 1)


def along_y(q, courant, half, slope):
    q_next = ahead(q, 1)
    edges = edge(pltpu.roll(q, 1, 1), q, q_next, ahead(q, 2))
    return face(
        courant, half, slope, pltpu.roll(edges, 1, 1), edges, ahead(edges, 1), q, q_next
    )


def step_kernel(low_row, high_row, base, last, q_ref, coef_ref, gathered_ref, east_ref, west_ref,
                from_west_ref, from_east_ref, rates_ref, *refs):
    if last:
        out_ref, forward_ref, flux_ref = refs
    else:
        out_ref, pack_east_ref, pack_west_ref, forward_ref, flux_ref = refs
    rows = list(range(low_row, high_row))
    rates = spun(rates_ref)
    lane = lax.broadcasted_iota(jnp.int32, (TR, LANES), 1)
    place = lane % 8

    def coef(k, at, row):
        return jnp.broadcast_to(coef_ref[k, pl.ds(at + spot(row), 1), :], (TR, LANES))

    def strip(k, at, value):
        courant = jnp.broadcast_to(gathered_ref[k, pl.ds(at, 1), :], (TR, LANES))
        size = jnp.abs(courant)
        return along_y(value, courant, 0.5 * size, 1.0 - size * (2.0 / 3.0))

    forward_ref[...] = jnp.zeros_like(forward_ref)
    flux_ref[...] = jnp.zeros_like(flux_ref)

    def down(k, carry):
        below = jnp.minimum(k + 1, NZ - 1)
        strip_w = strip(k, 64, jnp.where(place < 3, from_west_ref[k], east_ref[k]))
        strip_e = strip(k, 65, jnp.where(place < 5, west_ref[k], from_east_ref[k]))
        edges, flux_x = {}, {}

        def q(row):
            return q_ref[k, row + base]

        def edge_at(row):
            if row not in edges:
                edges[row] = edge(q(row - 1), q(row), q(row + 1), q(row + 2))
            return edges[row]

        def flux_at(row):
            if row not in flux_x:
                flux_x[row] = face(
                    coef(k, UX, row), coef(k, AX, row), coef(k, BX, row),
                    edge_at(row - 1), edge_at(row), edge_at(row + 1), q(row), q(row + 1),
                )
            return flux_x[row]

        for index, row in enumerate(rows):
            here = q(row)
            flux_y = along_y(here, coef(k, UY, row), coef(k, AY, row), coef(k, BY, row))
            at = 8 * (row + 3)
            low_end = pltpu.roll(strip_w, (LANES - at - 3) % LANES, 1)
            high_end = pltpu.roll(strip_e, (123 - at) % LANES, 1)
            flux_y = jnp.where(lane < 2, low_end, jnp.where(lane >= 125, high_end, flux_y))
            flux_south = pltpu.roll(jnp.where(lane == 127, low_end, flux_y), 1, 1)
            courant_z = coef(k, CZ, row)
            flux_z = courant_z * jnp.where(courant_z > 0, here, q_ref[below, row + base])
            advected = here - (
                (flux_at(row) - flux_at(row - 1)) + (flux_y - flux_south)
                + (flux_z - flux_ref[index])
            )
            flux_ref[index] = flux_z
            forward_ref[k + 1, index] = (
                advected + coef(k, LOWER, row) * forward_ref[k, index]
            ) * coef(k, INV, row)
        return carry

    lax.fori_loop(0, NZ, down, 0)
    flux_ref[...] = jnp.zeros_like(flux_ref)

    def up(step, carry):
        k = NZ - 1 - step
        own = {}
        for index, row in enumerate(rows):
            value = forward_ref[k + 1, index] - coef(k, RATIO, row) * flux_ref[index]
            flux_ref[index] = value
            if last:
                out_ref[pl.ds(k * 8 + row, TR, stride=NZ * 8), :] = value
            else:
                value = react(value, rates)
                out_ref[k, index] = value
                if 0 <= row < 8:
                    own[row] = value
        if not last:
            pack_east_ref[k], pack_west_ref[k] = pack(own.values(), own.keys())
        return carry

    lax.fori_loop(0, NZ, up, 0)


def transport(tracers, reaction, velocity, thickness, sea_mask, bottom, diffusivity):
    groups, stripes, count = lax.axis_size("dy"), lax.axis_size("dx") // XS, lax.axis_size("dx")
    x_index = (lax.axis_index("dx") % XS).astype(jnp.int32).reshape(1)

    def dx_pairs(forth, back):
        pairs = []
        for stripe in range(stripes):
            for source, target, far in forth:
                if 0 <= stripe + far < stripes and (far or stripe + 1 < stripes):
                    pairs.append((stripe * XS + source, (stripe + far) * XS + target))
            for source, target, far in back:
                if 0 <= stripe - far < stripes and (far or stripe > 0):
                    pairs.append((stripe * XS + source, (stripe - far) * XS + target))
        return pairs

    def collect_pairs(forth, back):
        pairs = []
        for stripe in range(stripes):
            if stripe > 0:
                pairs += [(stripe * XS + s, stripe * XS + t) for s, t in forth]
            if stripe + 1 < stripes:
                pairs += [(stripe * XS + s, stripe * XS + t) for s, t in back]
        return pairs

    sizes = [n for _, n in PIECES.values()]
    hi, lo, *far = call(
        first_kernel,
        [shape_of(NZ, HALO, TR, LANES)] * 2 + [shape_of(n, HALO, TR, LANES) for n in sizes],
        [x_index], [tracers.reshape(-1, LANES), sea_mask, bottom, reaction],
    )
    far = dict(zip(PIECES, far))
    own_piece = far.pop("O")
    far["A"] = lax.ppermute(far["A"], "dx", dx_pairs([(3, 2, 0)], [(0, 1, 0)]))
    far["B"] = lax.ppermute(far["B"], "dx", dx_pairs([(3, 0, 0)], [(0, 3, 0)]))
    far["C"] = lax.ppermute(far["C"], "dx", dx_pairs([(3, 1, 0)], [(0, 2, 0)]))
    velocity, thickness, sea_mask, bottom, diffusivity, far = lax.optimization_barrier(
        (velocity, thickness, sea_mask, bottom, diffusivity, far)
    )
    far["O"] = lax.ppermute(own_piece, "dx", dx_pairs([(3, 3, 1)], [(0, 0, 1)]))
    far["A"] = lax.ppermute(far["A"], "dx", dx_pairs([(2, 2, 1)], [(1, 1, 1)]))
    far["B"] = lax.ppermute(far["B"], "dx", dx_pairs([(0, 0, 1)], [(3, 3, 1)]))
    far["C"] = lax.ppermute(far["C"], "dx", dx_pairs([(1, 1, 1)], [(2, 2, 1)]))
    inside = [(i, i + 1) for i in range(count - 1) if i % XS != XS - 1]
    from_west = lax.ppermute(hi, "dx", inside)
    from_east = lax.ppermute(lo, "dx", [(b, a) for a, b in inside])
    far["O"] = lax.ppermute(far["O"], "dx", collect_pairs([(3, 0)], [(0, 3)]))
    far["A"] = lax.ppermute(far["A"], "dx", collect_pairs([(2, 0)], [(1, 3)]))
    far["C"] = lax.ppermute(far["C"], "dx", collect_pairs([(1, 0)], [(2, 3)]))

    levels = thickness.shape[0]
    first_level = lax.axis_index("group") * levels
    slab = 0.3 * jnp.tanh(velocity) * thickness[None]
    mix = lax.dynamic_slice_in_dim(diffusivity, first_level, levels, axis=0)
    depth = (sea_mask * bottom).astype(jnp.float32)
    own = jnp.concatenate([slab.reshape(-1, 8, LANES), mix, depth[None]], axis=0)
    forward = [(i, i + 1) for i in range(count - 1)]
    backward = [(b, a) for a, b in forward]
    rim_west = lax.ppermute(own[:, 4:], "dx", forward)
    rim_east = lax.ppermute(own[:, :4], "dx", backward)
    blocks = jnp.concatenate([own, rim_west, rim_east], axis=1)
    flux = blocks[: 3 * levels].reshape(3, levels, 16, LANES)
    mix, depth = blocks[3 * levels : 4 * levels], blocks[-1]
    north = [(i, i + 1) for i in range(groups - 1)]
    from_south = lax.ppermute(
        jnp.concatenate([flux[1, :, :, -1], depth[None, :, -1]], axis=0), "dy", north
    )
    depth_north = lax.ppermute(depth[None, :, 0], "dy", [(b, a) for a, b in north])[0]
    flux_south, depth_south = from_south[:-1], from_south[-1]
    level = (first_level + jnp.arange(levels)).astype(jnp.float32)[:, None, None]
    next_x = jnp.concatenate(
        [depth[1:8], depth[12:13], depth[9:12], depth[0:1], depth[13:16], depth[:1] * 0.0], axis=0
    )
    next_y = jnp.concatenate([depth[:, 1:], depth_north[:, None]], axis=1)
    courant_x = jnp.where(level < jnp.minimum(depth, next_x), flux[0], 0.0)
    courant_y = jnp.where(level < jnp.minimum(depth, next_y), flux[1], 0.0)
    courant_z = jnp.where(level + 1.0 < depth, flux[2], 0.0)
    coupling = jnp.where(level + 1.0 < depth, mix, 0.0)
    south = jnp.where(level[:, :, 0] < jnp.minimum(depth_south, depth[:, 0]), flux_south, 0.0)

    def strip_of(three):
        picked = jnp.concatenate([three[:, 9:12], three[:, 0:8], three[:, 12:15]], axis=1)
        picked = jnp.pad(picked, ((0, 0), (0, 2), (2, 3)))
        return picked.reshape(levels, 1, LANES)

    ends = [
        strip_of(jnp.concatenate([south[:, :, None], courant_y[:, :, :2]], axis=2)),
        strip_of(courant_y[:, :, -3:]),
        jnp.zeros((levels, 6, LANES), jnp.float32),
    ]
    table = jnp.concatenate([courant_x, courant_y, courant_z, coupling, *ends], axis=1)
    gathered = lax.all_gather(table, "group", axis=0, tiled=True)
    (coefs,) = call(coefficient_kernel, [shape_of(NZ, 160, LANES)], [], [gathered])

    def swap(east, west):
        return (
            lax.ppermute(east, "dy", north),
            lax.ppermute(west, "dy", [(b, a) for a, b in north]),
        )

    packs = [shape_of(NZ, TR, LANES)] * 2
    joined, east, west = call(
        join_kernel, [shape_of(NZ, 20, TR, LANES)] + packs, [x_index],
        [hi, lo, from_west, from_east] + [far[name] for name in PIECES],
    )

    def scratch(rows):
        return [
            pltpu.VMEM((NZ + 1, rows, TR, LANES), jnp.float32),
            pltpu.VMEM((rows, TR, LANES), jnp.float32),
        ]

    middle, east2, west2 = call(
        functools.partial(step_kernel, -3, 11, HALO, False),
        [shape_of(NZ, 14, TR, LANES)] + packs, [],
        [joined, coefs, gathered, east, west, *swap(east, west), reaction], scratch(14),
    )
    (out,) = call(
        functools.partial(step_kernel, 0, 8, 3, True),
        [shape_of(TR * NZ * 8, LANES)], [],
        [middle, coefs, gathered, east2, west2, *swap(east2, west2), reaction], scratch(8),
    )
    return out.reshape(TR, NZ, 8, LANES)


def solution(mesh):
    placed = (
        P("group", None, "dx", "dy"),
        P("group", None),
        P(None, "group", "dx", "dy"),
        P("group", "dx", "dy"),
        P("dx", "dy"),
        P("dx", "dy"),
        P(None, "dx", "dy"),
    )
    return jax.shard_map(
        transport,
        mesh=mesh,
        in_specs=placed,
        out_specs=P("group", None, "dx", "dy"),
        check_vma=False,
    )
```

```python
import functools

import jax
import jax.numpy as jnp
from jax import lax
from jax.experimental import pallas as pl
from jax.experimental.pallas import tpu as pltpu
from jax.sharding import PartitionSpec as P

INTERPRET = False
XS = 4
NZ = 32
TR = 8
LANES = 128
HALO = 6
VMEM_LIMIT = 24 << 20
UNROLL = 2
PIECES = {"O": (0, 8), "A": (8, 8), "B": (16, 9), "C": (25, 7)}


def spot(row):
    if row < 0:
        return 12 + row
    return row if row < 8 else row + 4


def vmem(count):
    return [pl.BlockSpec(memory_space=pltpu.VMEM)] * count


def shape_of(*dims):
    if INTERPRET:
        return jax.ShapeDtypeStruct(dims, jnp.float32)
    return pltpu.VMEM(dims, jnp.float32)


def stored(value):
    return value if INTERPRET else pltpu.with_memory_space_constraint(value, pltpu.HBM)


def kept(value):
    return value if INTERPRET else pltpu.with_memory_space_constraint(value, pltpu.VMEM)


def fetched(body, skip, count):
    def wrapped(*refs):
        *refs, arrivals = refs
        sources, places = refs[skip : skip + count], refs[len(refs) - count :]
        copies = [
            pltpu.make_async_copy(source, place, arrivals.at[index])
            for index, (source, place) in enumerate(zip(sources, places))
        ]
        for copy in copies:
            copy.start()
        for copy in copies:
            copy.wait()
        body(*refs[:skip], *places, *refs[skip + count : len(refs) - count])

    return wrapped if count else body


def call(body, outs, scalars, arrays, scratch=(), arguments=()):
    return pl.pallas_call(
        fetched(body, len(scalars), len(arguments)),
        out_shape=outs,
        in_specs=[pl.BlockSpec(memory_space=pltpu.SMEM)] * len(scalars)
        + [pl.BlockSpec(memory_space=pltpu.HBM)] * len(arguments)
        + vmem(len(arrays)),
        out_specs=vmem(len(outs)),
        scratch_shapes=list(scratch)
        + [pltpu.VMEM(value.shape, value.dtype) for value in arguments]
        + [pltpu.SemaphoreType.DMA((len(arguments),))] * bool(arguments),
        compiler_params=pltpu.CompilerParams(vmem_limit_bytes=VMEM_LIMIT),
        interpret=INTERPRET,
    )(*scalars, *map(stored, arguments), *map(kept, arrays))


def spun(rates_ref):
    rates = rates_ref[...]
    tracer = lax.broadcasted_iota(jnp.int32, (TR, TR), 0)
    other = lax.broadcasted_iota(jnp.int32, (TR, TR), 1)
    spins = []
    for shift in range(TR):
        picked = jnp.where(other == (tracer + TR - shift) % TR, rates, 0.0)
        spins.append(jnp.broadcast_to(jnp.sum(picked, axis=1, keepdims=True), (TR, LANES)))
    return spins


def react(value, rates):
    total = rates[0] * value
    for shift in range(1, TR):
        total = total + rates[shift] * pltpu.roll(value, shift, 0)
    return value + value * total


def first_kernel(x_ref, tracers_ref, sea_ref, bottom_ref, rates_ref, hi_ref, lo_ref, *far_refs):
    depth = sea_ref[...] * bottom_ref[...]
    depths = [jnp.broadcast_to(depth[row : row + 1], (TR, LANES)) for row in range(8)]
    rates = spun(rates_ref)

    def level(k, carry):
        for row in range(8):
            value = tracers_ref[pl.ds(k * 8 + row, TR, stride=NZ * 8), :]
            value = react(jnp.where(k < depths[row], value, 0.0), rates)
            if row < HALO:
                lo_ref[k, row] = value
            if row >= 8 - HALO:
                hi_ref[k, row - (8 - HALO)] = value
        return carry

    lax.fori_loop(0, NZ, level, 0)
    for far_ref, (first, count) in zip(far_refs, PIECES.values()):

        @pl.when(x_ref[0] == XS - 1)
        def _():
            far_ref[...] = hi_ref[first : first + count]

        @pl.when(x_ref[0] != XS - 1)
        def _():
            far_ref[...] = lo_ref[first : first + count]


def pack(values, rows):
    lane = lax.broadcasted_iota(jnp.int32, (TR, LANES), 1)
    slot = lane // 8
    east = west = jnp.zeros((TR, LANES), jnp.float32)
    for value, row in zip(values, rows):
        place = 8 * (row + 3)
        here = slot == row + 3
        east = jnp.where(here, pltpu.roll(value, (place + 3) % LANES, 1), east)
        west = jnp.where(here, pltpu.roll(value, (place + 5) % LANES, 1), west)
    return east, west


def join_kernel(x_ref, hi_ref, lo_ref, west_ref, east_ref, *refs):
    pieces, (all_ref, pack_east_ref, pack_west_ref) = refs[:4], refs[4:]
    for near_ref, owner, base in ((west_ref, 0, 0), (east_ref, XS - 1, HALO + 8)):

        @pl.when(x_ref[0] == owner)
        def _():
            for piece_ref, (first, count) in zip(pieces, PIECES.values()):
                all_ref[first : first + count, base : base + HALO] = piece_ref[...]

        @pl.when(x_ref[0] != owner)
        def _():
            all_ref[:, base : base + HALO] = near_ref[...]

    all_ref[:, HALO : 2 * HALO] = lo_ref[...]
    all_ref[:, 2 * HALO : 2 * HALO + 2] = hi_ref[:, HALO - 2 : HALO]
    rows = list(range(-3, 11))

    def level(k, carry):
        packed = pack([all_ref[k, row + HALO] for row in rows], rows)
        pack_east_ref[k], pack_west_ref[k] = packed
        return carry

    lax.fori_loop(0, NZ, level, 0)


UX, AX, BX, UY, AY, BY, CZ, INV, RATIO, LOWER = range(0, 160, 16)
ENDS = 160


def own_kernel(group_ref, x_ref, sea_ref, bottom_ref, mix_ref, slab_ref, own_ref, *rim_refs):
    levels = slab_ref.shape[1]
    first_level = group_ref[0] * levels
    for kind in range(3):
        own_ref[kind * levels : (kind + 1) * levels] = slab_ref[kind]
    own_ref[3 * levels : 4 * levels] = mix_ref[pl.ds(first_level, levels)]
    own_ref[4 * levels] = (sea_ref[...] * bottom_ref[...]).astype(jnp.float32)
    low_ref, high_ref, far_ref = rim_refs
    low_ref[...] = jnp.zeros_like(low_ref)
    high_ref[...] = jnp.zeros_like(high_ref)
    for item in range(own_ref.shape[0]):
        place = pl.ds(4 * (item % 2), 4)
        low_ref[item // 2, place] = own_ref[item, 0:4]
        high_ref[item // 2, place] = own_ref[item, 4:8]
    far_ref[...] = jnp.where(x_ref[0] == XS - 1, high_ref[...], low_ref[...])


def blocks_kernel(x_ref, own_ref, west_ref, east_ref, far_ref, blocks_ref, north_ref, south_ref):
    items = own_ref.shape[0]
    levels = items // 4
    blocks_ref[:, 0:8] = own_ref[...]
    for item in range(items):
        place = pl.ds(4 * (item % 2), 4)
        far = far_ref[item // 2, place]
        blocks_ref[item, 8:12] = jnp.where(x_ref[0] == 0, far, west_ref[item // 2, place])
        blocks_ref[item, 12:16] = jnp.where(x_ref[0] == XS - 1, far, east_ref[item // 2, place])
    for index, item in enumerate([*range(levels, 2 * levels), items - 1]):
        north_ref[index] = jnp.broadcast_to(
            blocks_ref[item][:, LANES - 1 : LANES], (16, LANES)
        )
    south_ref[0] = jnp.broadcast_to(blocks_ref[items - 1][:, 0:1], (16, LANES))


def table_kernel(group_ref, blocks_ref, south_ref, north_ref, table_ref, next_ref):
    items = blocks_ref.shape[0]
    levels = items // 4
    lane = lax.broadcasted_iota(jnp.int32, (16, LANES), 1)
    slot = lax.broadcasted_iota(jnp.int32, (8, LANES), 1) // 8
    depth = blocks_ref[items - 1]
    for target, source, count in ((0, 1, 7), (7, 12, 1), (8, 9, 3), (11, 0, 1), (12, 13, 3)):
        next_ref[target : target + count] = blocks_ref[items - 1, source : source + count]
    next_ref[15:16] = jnp.zeros((1, LANES), jnp.float32)
    depth_x = jnp.minimum(depth, next_ref[...])
    depth_y = jnp.minimum(
        depth, jnp.where(lane == LANES - 1, north_ref[0], pltpu.roll(depth, LANES - 1, 1))
    )
    depth_south = jnp.minimum(south_ref[levels], jnp.broadcast_to(depth[:, 0:1], (16, LANES)))
    table_ref[...] = jnp.zeros_like(table_ref)
    for index in range(levels):
        level = (group_ref[0] * levels + index).astype(jnp.float32)
        courant_y = jnp.where(level < depth_y, blocks_ref[levels + index], 0.0)
        table_ref[index, 0:16] = jnp.where(level < depth_x, blocks_ref[index], 0.0)
        table_ref[index, 16:32] = courant_y
        wet_below = level + 1.0 < depth
        table_ref[index, 32:48] = jnp.where(wet_below, blocks_ref[2 * levels + index], 0.0)
        table_ref[index, 48:64] = jnp.where(wet_below, blocks_ref[3 * levels + index], 0.0)
        south = jnp.where(level < depth_south, south_ref[index], 0.0)
        next_ref[...] = jnp.where(lane == LANES - 1, south, courant_y)
        low = high = jnp.zeros((8, LANES), jnp.float32)
        for row in range(-3, 11):
            at = 8 * (row + 3)
            here = slot == row + 3
            place = pl.ds(spot(row), 1)
            low_row = jnp.broadcast_to(next_ref[place], (8, LANES))
            high_row = jnp.broadcast_to(table_ref[index, pl.ds(16 + spot(row), 1)], (8, LANES))
            low = jnp.where(here, pltpu.roll(low_row, (at + 3) % LANES, 1), low)
            high = jnp.where(here, pltpu.roll(high_row, (at + 5) % LANES, 1), high)
        table_ref[index, 64:65] = low[0:1]
        table_ref[index, 65:66] = high[0:1]


def coefficient_kernel(order, group_ref, *refs):
    pieces, out_ref = refs[:-1], refs[-1]
    levels = pieces[0].shape[0]
    for (flip, turn), piece_ref in zip(order, pieces):
        owner = (group_ref[0] // 2 + turn) % (len(order) // 2) * 2 + (group_ref[0] % 2 + flip) % 2

        def spread(index, carry):
            k = owner * levels + index
            for source, at in ((0, UX), (16, UY)):
                courant = piece_ref[index, source : source + 16]
                size = jnp.abs(courant)
                out_ref[k, at : at + 16] = courant
                out_ref[k, at + 16 : at + 32] = 0.5 * size
                out_ref[k, at + 32 : at + 48] = 1.0 - size * (2.0 / 3.0)
            out_ref[k, CZ : CZ + 16] = piece_ref[index, 32:48]
            out_ref[k, INV : INV + 16] = piece_ref[index, 48:64]
            out_ref[k, ENDS : ENDS + 8] = piece_ref[index, 64:72]
            return carry

        lax.fori_loop(0, levels, spread, 0)

    def level(k, carry):
        ratio_before, lower = carry
        upper = out_ref[k, INV : INV + 16]
        inverse = 1.0 / (1.0 + lower + upper + lower * ratio_before)
        ratio = -upper * inverse
        out_ref[k, INV : INV + 16] = inverse
        out_ref[k, RATIO : RATIO + 16] = ratio
        out_ref[k, LOWER : LOWER + 16] = lower
        return ratio, upper

    zero = jnp.zeros((16, LANES), jnp.float32)
    lax.fori_loop(0, NZ, level, (zero, zero))


def edge(outer_lo, inner_lo, inner_hi, outer_hi):
    value = 7.0 / 12.0 * (inner_lo + inner_hi) - 1.0 / 12.0 * (outer_lo + outer_hi)
    return jnp.minimum(
        jnp.maximum(value, jnp.minimum(inner_lo, inner_hi)), jnp.maximum(inner_lo, inner_hi)
    )


def face(courant, half, slope, low_edge, near, high_edge, low_cell, high_cell):
    positive = courant > 0
    far = jnp.where(positive, low_edge, high_edge)
    cell = jnp.where(positive, low_cell, high_cell)
    curve = 6.0 * cell - 3.0 * (near + far)
    return courant * (near - half * ((near - far) - slope * curve))


def ahead(value, count):
    return pltpu.roll(value, (LANES - count) % LANES, 1)


def along_y(q, courant, half, slope):
    q_next = ahead(q, 1)
    edges = edge(pltpu.roll(q, 1, 1), q, q_next, ahead(q, 2))
    return face(
        courant, half, slope, pltpu.roll(edges, 1, 1), edges, ahead(edges, 1), q, q_next
    )


def step_kernel(low_row, high_row, base, last, q_ref, coef_ref, east_ref, west_ref,
                from_west_ref, from_east_ref, rates_ref, *refs):
    if last:
        out_ref, forward_ref, flux_ref = refs
    else:
        out_ref, pack_east_ref, pack_west_ref, forward_ref, flux_ref = refs
    rows = list(range(low_row, high_row))
    rates = spun(rates_ref)
    lane = lax.broadcasted_iota(jnp.int32, (TR, LANES), 1)
    place = lane % 8

    def coef(k, at, row):
        return jnp.broadcast_to(coef_ref[k, pl.ds(at + spot(row), 1), :], (TR, LANES))

    def strip(k, at, value):
        courant = jnp.broadcast_to(coef_ref[k, pl.ds(ENDS + at, 1), :], (TR, LANES))
        size = jnp.abs(courant)
        return along_y(value, courant, 0.5 * size, 1.0 - size * (2.0 / 3.0))

    forward_ref[...] = jnp.zeros_like(forward_ref)
    flux_ref[...] = jnp.zeros_like(flux_ref)

    def down(k):
        below = jnp.minimum(k + 1, NZ - 1)
        strip_w = strip(k, 0, jnp.where(place < 3, from_west_ref[k], east_ref[k]))
        strip_e = strip(k, 1, jnp.where(place < 5, west_ref[k], from_east_ref[k]))
        edges, flux_x = {}, {}

        def q(row):
            return q_ref[k, row + base]

        def edge_at(row):
            if row not in edges:
                edges[row] = edge(q(row - 1), q(row), q(row + 1), q(row + 2))
            return edges[row]

        def flux_at(row):
            if row not in flux_x:
                flux_x[row] = face(
                    coef(k, UX, row), coef(k, AX, row), coef(k, BX, row),
                    edge_at(row - 1), edge_at(row), edge_at(row + 1), q(row), q(row + 1),
                )
            return flux_x[row]

        for index, row in enumerate(rows):
            here = q(row)
            flux_y = along_y(here, coef(k, UY, row), coef(k, AY, row), coef(k, BY, row))
            at = 8 * (row + 3)
            low_end = pltpu.roll(strip_w, (LANES - at - 3) % LANES, 1)
            high_end = pltpu.roll(strip_e, (123 - at) % LANES, 1)
            flux_y = jnp.where(lane < 2, low_end, jnp.where(lane >= 125, high_end, flux_y))
            flux_south = pltpu.roll(jnp.where(lane == 127, low_end, flux_y), 1, 1)
            courant_z = coef(k, CZ, row)
            flux_z = courant_z * jnp.where(courant_z > 0, here, q_ref[below, row + base])
            advected = here - (
                (flux_at(row) - flux_at(row - 1)) + (flux_y - flux_south)
                + (flux_z - flux_ref[index])
            )
            flux_ref[index] = flux_z
            forward_ref[k + 1, index] = (
                advected + coef(k, LOWER, row) * forward_ref[k, index]
            ) * coef(k, INV, row)

    @pl.loop(0, NZ // UNROLL)
    def _(part):
        for index in range(UNROLL):
            down(part * UNROLL + index)

    flux_ref[...] = jnp.zeros_like(flux_ref)

    def up(k):
        own = {}
        for index, row in enumerate(rows):
            value = forward_ref[k + 1, index] - coef(k, RATIO, row) * flux_ref[index]
            flux_ref[index] = value
            if last:
                out_ref[pl.ds(k * 8 + row, TR, stride=NZ * 8), :] = value
            else:
                value = react(value, rates)
                out_ref[k, index] = value
                if 0 <= row < 8:
                    own[row] = value
        if not last:
            pack_east_ref[k], pack_west_ref[k] = pack(own.values(), own.keys())

    @pl.loop(0, NZ // UNROLL)
    def _(part):
        for index in range(UNROLL):
            up(NZ - 1 - part * UNROLL - index)


def transport(tracers, reaction, velocity, thickness, sea_mask, bottom, diffusivity):
    groups, stripes, count = lax.axis_size("dy"), lax.axis_size("dx") // XS, lax.axis_size("dx")
    group = lax.axis_index("group").astype(jnp.int32).reshape(1)
    x_index = (lax.axis_index("dx") % XS).astype(jnp.int32).reshape(1)

    def dx_pairs(forth, back):
        pairs = []
        for stripe in range(stripes):
            for source, target, far in forth:
                if 0 <= stripe + far < stripes and (far or stripe + 1 < stripes):
                    pairs.append((stripe * XS + source, (stripe + far) * XS + target))
            for source, target, far in back:
                if 0 <= stripe - far < stripes and (far or stripe > 0):
                    pairs.append((stripe * XS + source, (stripe - far) * XS + target))
        return pairs

    def collect_pairs(forth, back):
        pairs = []
        for stripe in range(stripes):
            if stripe > 0:
                pairs += [(stripe * XS + s, stripe * XS + t) for s, t in forth]
            if stripe + 1 < stripes:
                pairs += [(stripe * XS + s, stripe * XS + t) for s, t in back]
        return pairs

    sizes = [n for _, n in PIECES.values()]
    hi, lo, *far = call(
        first_kernel,
        [shape_of(NZ, HALO, TR, LANES)] * 2 + [shape_of(n, HALO, TR, LANES) for n in sizes],
        [x_index], [], (), [tracers.reshape(-1, LANES), sea_mask, bottom, reaction],
    )
    velocity, thickness, sea_mask, bottom, diffusivity, far = lax.optimization_barrier(
        (velocity, thickness, sea_mask, bottom, diffusivity, far)
    )
    far = dict(zip(PIECES, far))
    far["A"] = lax.ppermute(far["A"], "dx", dx_pairs([(3, 2, 0)], [(0, 1, 0)]))
    far["B"] = lax.ppermute(far["B"], "dx", dx_pairs([(3, 0, 0)], [(0, 3, 0)]))
    far["C"] = lax.ppermute(far["C"], "dx", dx_pairs([(3, 1, 0)], [(0, 2, 0)]))
    far["O"] = lax.ppermute(far["O"], "dx", dx_pairs([(3, 3, 1)], [(0, 0, 1)]))
    far["A"] = lax.ppermute(far["A"], "dx", dx_pairs([(2, 2, 1)], [(1, 1, 1)]))
    far["B"] = lax.ppermute(far["B"], "dx", dx_pairs([(0, 0, 1)], [(3, 3, 1)]))
    far["C"] = lax.ppermute(far["C"], "dx", dx_pairs([(1, 1, 1)], [(2, 2, 1)]))
    inside = [(i, i + 1) for i in range(count - 1) if i % XS != XS - 1]
    outside = [(b, a) for a, b in inside]
    from_west = lax.ppermute(hi, "dx", inside)
    from_east = lax.ppermute(lo, "dx", outside)
    far["O"] = lax.ppermute(far["O"], "dx", collect_pairs([(3, 0)], [(0, 3)]))
    far["A"] = lax.ppermute(far["A"], "dx", collect_pairs([(2, 0)], [(1, 3)]))
    far["C"] = lax.ppermute(far["C"], "dx", collect_pairs([(1, 0)], [(2, 3)]))

    levels = thickness.shape[0]
    items = 4 * levels + 1
    slab = 0.3 * jnp.tanh(velocity) * thickness[None]
    rim = shape_of((items + 1) // 2, 8, LANES)

    own, rim_low, rim_high, rim_far = call(
        own_kernel, [shape_of(items, 8, LANES)] + [rim] * 3, [group, x_index], [slab], (),
        [sea_mask, bottom, diffusivity],
    )
    rim_west = lax.ppermute(rim_high, "dx", inside)
    rim_east = lax.ppermute(rim_low, "dx", outside)
    swapped = [(i, i + 1) for i in range(count - 1) if i % XS == XS - 1]
    rim_far = lax.ppermute(rim_far, "dx", swapped + [(b, a) for a, b in swapped])
    blocks, to_north, to_south = call(
        blocks_kernel,
        [shape_of(items, 16, LANES), shape_of(levels + 1, 16, LANES), shape_of(1, 16, LANES)],
        [x_index], [own, rim_west, rim_east, rim_far],
    )
    north = [(i, i + 1) for i in range(groups - 1)]
    south = [(b, a) for a, b in north]
    (table,) = call(
        table_kernel, [shape_of(levels, 72, LANES)], [group],
        [blocks, lax.ppermute(to_north, "dy", north), lax.ppermute(to_south, "dy", south)],
        [pltpu.VMEM((16, LANES), jnp.float32)],
    )
    members = lax.axis_size("group")

    def gather(value, flip, turn):
        pairs = [((i + 2 * turn) % members ^ flip, i) for i in range(members)]
        return lax.ppermute(value, "group", pairs)

    turns = [1, 3, 2] if members == 8 else list(range(1, members // 2))
    along = [table] + [gather(table, 0, turn) for turn in turns]
    across = [gather(value, 1, 0) for value in along]
    order = [(flip, turn) for flip in (0, 1) for turn in [0] + turns]
    (coefs,) = call(
        functools.partial(coefficient_kernel, order), [shape_of(NZ, ENDS + 8, LANES)],
        [group], along + across,
    )

    def swap(east, west):
        return lax.ppermute(east, "dy", north), lax.ppermute(west, "dy", south)

    packs = [shape_of(NZ, TR, LANES)] * 2
    joined, east, west = call(
        join_kernel, [shape_of(NZ, 20, TR, LANES)] + packs, [x_index],
        [hi, lo, from_west, from_east] + [far[name] for name in PIECES],
    )

    def scratch(rows):
        return [
            pltpu.VMEM((NZ + 1, rows, TR, LANES), jnp.float32),
            pltpu.VMEM((rows, TR, LANES), jnp.float32),
        ]

    middle, east2, west2 = call(
        functools.partial(step_kernel, -3, 11, HALO, False),
        [shape_of(NZ, 14, TR, LANES)] + packs, [],
        [joined, coefs, east, west, *swap(east, west), reaction], scratch(14),
    )
    (out,) = call(
        functools.partial(step_kernel, 0, 8, 3, True),
        [jax.ShapeDtypeStruct((TR * NZ * 8, LANES), jnp.float32)], [],
        [middle, coefs, east2, west2, *swap(east2, west2), reaction], scratch(8),
    )
    return out.reshape(TR, NZ, 8, LANES)


def solution(mesh):
    placed = (
        P("group", None, "dx", "dy"),
        P("group", None),
        P(None, "group", "dx", "dy"),
        P("group", "dx", "dy"),
        P("dx", "dy"),
        P("dx", "dy"),
        P(None, "dx", "dy"),
    )
    return jax.shard_map(
        transport,
        mesh=mesh,
        in_specs=placed,
        out_specs=P("group", None, "dx", "dy"),
        check_vma=False,
    )
```

```python
import functools

import jax
import jax.numpy as jnp
from jax import lax
from jax.experimental import pallas as pl
from jax.experimental.pallas import tpu as pltpu
from jax.sharding import PartitionSpec as P

INTERPRET = False
XS = 4
NZ = 32
TR = 8
LANES = 128
HALO = 6
VMEM_LIMIT = 24 << 20
UNROLL = 2
PIECES = {"O": (0, 8), "A": (8, 10), "B": (18, 8), "C": (26, 6)}


def spot(row):
    if row < 0:
        return 12 + row
    return row if row < 8 else row + 4


def vmem(count):
    return [pl.BlockSpec(memory_space=pltpu.VMEM)] * count


def shape_of(*dims):
    if INTERPRET:
        return jax.ShapeDtypeStruct(dims, jnp.float32)
    return pltpu.VMEM(dims, jnp.float32)


def stored(value):
    return value if INTERPRET else pltpu.with_memory_space_constraint(value, pltpu.HBM)


def kept(value):
    return value if INTERPRET else pltpu.with_memory_space_constraint(value, pltpu.VMEM)


def fetched(body, skip, count):
    def wrapped(*refs):
        *refs, arrivals = refs
        sources, places = refs[skip : skip + count], refs[len(refs) - count :]
        copies = [
            pltpu.make_async_copy(source, place, arrivals.at[index])
            for index, (source, place) in enumerate(zip(sources, places))
        ]
        for copy in copies:
            copy.start()
        for copy in copies:
            copy.wait()
        body(*refs[:skip], *places, *refs[skip + count : len(refs) - count])

    return wrapped if count else body


def call(body, outs, scalars, arrays, scratch=(), arguments=()):
    return pl.pallas_call(
        fetched(body, len(scalars), len(arguments)),
        out_shape=outs,
        in_specs=[pl.BlockSpec(memory_space=pltpu.SMEM)] * len(scalars)
        + [pl.BlockSpec(memory_space=pltpu.HBM)] * len(arguments)
        + vmem(len(arrays)),
        out_specs=vmem(len(outs)),
        scratch_shapes=list(scratch)
        + [pltpu.VMEM(value.shape, value.dtype) for value in arguments]
        + [pltpu.SemaphoreType.DMA((len(arguments),))] * bool(arguments),
        compiler_params=pltpu.CompilerParams(vmem_limit_bytes=VMEM_LIMIT),
        interpret=INTERPRET,
    )(*scalars, *map(stored, arguments), *map(kept, arrays))


def spun(rates_ref):
    rates = rates_ref[...]
    tracer = lax.broadcasted_iota(jnp.int32, (TR, TR), 0)
    other = lax.broadcasted_iota(jnp.int32, (TR, TR), 1)
    spins = []
    for shift in range(TR):
        picked = jnp.where(other == (tracer + TR - shift) % TR, rates, 0.0)
        spins.append(jnp.broadcast_to(jnp.sum(picked, axis=1, keepdims=True), (TR, LANES)))
    return spins


def react(value, rates):
    total = rates[0] * value
    for shift in range(1, TR):
        total = total + rates[shift] * pltpu.roll(value, shift, 0)
    return value + value * total


def first_kernel(x_ref, tracers_ref, sea_ref, bottom_ref, rates_ref, hi_ref, lo_ref, *far_refs):
    depth = sea_ref[...] * bottom_ref[...]
    depths = [jnp.broadcast_to(depth[row : row + 1], (TR, LANES)) for row in range(8)]
    rates = spun(rates_ref)

    def level(k, carry):
        for row in range(8):
            value = tracers_ref[pl.ds(k * 8 + row, TR, stride=NZ * 8), :]
            value = react(jnp.where(k < depths[row], value, 0.0), rates)
            if row < HALO:
                lo_ref[k, row] = value
            if row >= 8 - HALO:
                hi_ref[k, row - (8 - HALO)] = value
        return carry

    lax.fori_loop(0, NZ, level, 0)
    for far_ref, (first, count) in zip(far_refs, PIECES.values()):

        @pl.when(x_ref[0] == XS - 1)
        def _():
            far_ref[...] = hi_ref[first : first + count]

        @pl.when(x_ref[0] != XS - 1)
        def _():
            far_ref[...] = lo_ref[first : first + count]


def pack(values, rows, east=None, west=None):
    lane = lax.broadcasted_iota(jnp.int32, (TR, LANES), 1)
    slot = lane // 8
    if east is None:
        east = west = jnp.zeros((TR, LANES), jnp.float32)
    for value, row in zip(values, rows):
        place = 8 * (row + 3)
        here = slot == row + 3
        east = jnp.where(here, pltpu.roll(value, (place + 3) % LANES, 1), east)
        west = jnp.where(here, pltpu.roll(value, (place + 5) % LANES, 1), west)
    return east, west


HALF = NZ // 2


def merge(message_ref, k, value, from_low):
    place = lax.broadcasted_iota(jnp.int32, (TR, LANES), 1) % 8
    mine = (place < 4) == from_low
    slot = k % HALF
    moved = pltpu.roll(value, 4 if from_low else LANES - 4, 1)
    message_ref[slot] = jnp.where(k >= HALF, moved, jnp.where(mine, value, message_ref[slot]))


def received(message_ref, k, from_low):
    value = message_ref[k % HALF]
    return jnp.where(k >= HALF, pltpu.roll(value, LANES - 4 if from_low else 4, 1), value)


def ends_kernel(hi_ref, lo_ref, east_ref, west_ref):
    def level(k, carry):
        values = [lo_ref[k, row] for row in range(HALO)]
        values += [hi_ref[k, row] for row in range(2 * HALO - 8, HALO)]
        east_ref[k], west_ref[k] = pack(values, range(8))
        return carry

    lax.fori_loop(0, NZ, level, 0)


def join_kernel(x_ref, hi_ref, lo_ref, west_ref, east_ref, *refs):
    pieces, (coef_ref, own_east_ref, own_west_ref, all_ref, *pack_refs) = refs[:4], refs[4:]
    pack_east_ref, pack_west_ref, send_east_ref, send_west_ref = pack_refs
    place = lax.broadcasted_iota(jnp.int32, (TR, LANES), 1) % 8
    for near_ref, owner, base in ((west_ref, 0, 0), (east_ref, XS - 1, HALO + 8)):

        @pl.when(x_ref[0] == owner)
        def _():
            for piece_ref, (first, count) in zip(pieces, PIECES.values()):
                all_ref[first : first + count, base : base + HALO] = piece_ref[...]

        @pl.when(x_ref[0] != owner)
        def _():
            all_ref[:, base : base + HALO] = near_ref[...]

    all_ref[:, HALO : 2 * HALO] = lo_ref[...]
    all_ref[:, 2 * HALO : 2 * HALO + 2] = hi_ref[:, HALO - 2 : HALO]
    rows = [-3, -2, -1, 8, 9, 10]

    def level(step, carry):
        k = NZ - 1 - step
        east, west = pack(
            [all_ref[k, row + HALO] for row in rows], rows, own_east_ref[k], own_west_ref[k]
        )
        pack_east_ref[k], pack_west_ref[k] = east, west
        last_face = jnp.broadcast_to(coef_ref[k, pl.ds(ENDS + 1, 1)], (TR, LANES))
        first_wet = jnp.broadcast_to(coef_ref[k, pl.ds(ENDS, 1)], (TR, LANES))
        last_face = pltpu.roll(last_face, LANES - 1, 1)
        first_wet = pltpu.roll(first_wet, 2, 1)
        merge(send_east_ref, k, jnp.where(place < 3, east, last_face), True)
        merge(send_west_ref, k, jnp.where(place < 5, first_wet, west), False)
        return carry

    lax.fori_loop(0, NZ, level, 0)


UX, AX, BX, UY, AY, BY, CZ, INV, RATIO, LOWER = range(0, 160, 16)
ENDS = 160


def own_kernel(group_ref, x_ref, sea_ref, bottom_ref, mix_ref, slab_ref, own_ref, *rim_refs):
    levels = slab_ref.shape[1]
    first_level = group_ref[0] * levels
    for kind in range(3):
        own_ref[kind * levels : (kind + 1) * levels] = slab_ref[kind]
    own_ref[3 * levels : 4 * levels] = mix_ref[pl.ds(first_level, levels)]
    own_ref[4 * levels] = (sea_ref[...] * bottom_ref[...]).astype(jnp.float32)
    low_ref, high_ref, far_ref = rim_refs
    low_ref[...] = jnp.zeros_like(low_ref)
    high_ref[...] = jnp.zeros_like(high_ref)
    for item in range(own_ref.shape[0]):
        place = pl.ds(4 * (item % 2), 4)
        low_ref[item // 2, place] = own_ref[item, 0:4]
        high_ref[item // 2, place] = own_ref[item, 4:8]
    far_ref[...] = jnp.where(x_ref[0] == XS - 1, high_ref[...], low_ref[...])


def table_kernel(group_ref, x_ref, own_ref, west_ref, east_ref, far_ref, table_ref, blocks_ref,
                 next_ref):
    items = own_ref.shape[0]
    levels = items // 4
    blocks_ref[:, 0:8] = own_ref[...]
    for item in range(items):
        place = pl.ds(4 * (item % 2), 4)
        far = far_ref[item // 2, place]
        blocks_ref[item, 8:12] = jnp.where(x_ref[0] == 0, far, west_ref[item // 2, place])
        blocks_ref[item, 12:16] = jnp.where(x_ref[0] == XS - 1, far, east_ref[item // 2, place])
    lane = lax.broadcasted_iota(jnp.int32, (16, LANES), 1)
    slot = lax.broadcasted_iota(jnp.int32, (8, LANES), 1) // 8
    depth = blocks_ref[items - 1]
    for target, source, count in ((0, 1, 7), (7, 12, 1), (8, 9, 3), (11, 0, 1), (12, 13, 3)):
        next_ref[target : target + count] = blocks_ref[items - 1, source : source + count]
    next_ref[15:16] = jnp.zeros((1, LANES), jnp.float32)
    depth_x = jnp.minimum(depth, next_ref[...])
    depth_y = jnp.where(
        lane == LANES - 1, depth, jnp.minimum(depth, pltpu.roll(depth, LANES - 1, 1))
    )
    depth_first = jnp.broadcast_to(depth[:, 0:1], (16, LANES))
    table_ref[...] = jnp.zeros_like(table_ref)
    for index in range(levels):
        level = (group_ref[0] * levels + index).astype(jnp.float32)
        courant_y = jnp.where(level < depth_y, blocks_ref[levels + index], 0.0)
        table_ref[index, 0:16] = jnp.where(level < depth_x, blocks_ref[index], 0.0)
        table_ref[index, 16:32] = courant_y
        wet_below = level + 1.0 < depth
        table_ref[index, 32:48] = jnp.where(wet_below, blocks_ref[2 * levels + index], 0.0)
        table_ref[index, 48:64] = jnp.where(wet_below, blocks_ref[3 * levels + index], 0.0)
        wet_first = jnp.where(level < depth_first, 1.0, 0.0)
        next_ref[...] = jnp.where(lane == LANES - 1, wet_first, courant_y)
        low = high = jnp.zeros((8, LANES), jnp.float32)
        for row in range(-3, 11):
            at = 8 * (row + 3)
            here = slot == row + 3
            place = pl.ds(spot(row), 1)
            low_row = jnp.broadcast_to(next_ref[place], (8, LANES))
            high_row = jnp.broadcast_to(table_ref[index, pl.ds(16 + spot(row), 1)], (8, LANES))
            low = jnp.where(here, pltpu.roll(low_row, (at + 3) % LANES, 1), low)
            high = jnp.where(here, pltpu.roll(high_row, (at + 5) % LANES, 1), high)
        table_ref[index, 64:65] = low[0:1]
        table_ref[index, 65:66] = high[0:1]


def coefficient_kernel(order, group_ref, *refs):
    pieces, out_ref = refs[:-1], refs[-1]
    levels = pieces[0].shape[0]
    for (flip, turn), piece_ref in zip(order, pieces):
        owner = (group_ref[0] // 2 + turn) % (len(order) // 2) * 2 + (group_ref[0] % 2 + flip) % 2

        def spread(index, carry):
            k = owner * levels + index
            for source, at in ((0, UX), (16, UY)):
                courant = piece_ref[index, source : source + 16]
                size = jnp.abs(courant)
                out_ref[k, at : at + 16] = courant
                out_ref[k, at + 16 : at + 32] = 0.5 * size
                out_ref[k, at + 32 : at + 48] = 1.0 - size * (2.0 / 3.0)
            out_ref[k, CZ : CZ + 16] = piece_ref[index, 32:48]
            out_ref[k, INV : INV + 16] = piece_ref[index, 48:64]
            out_ref[k, ENDS : ENDS + 8] = piece_ref[index, 64:72]
            return carry

        lax.fori_loop(0, levels, spread, 0)

    def level(k, carry):
        ratio_before, lower = carry
        upper = out_ref[k, INV : INV + 16]
        inverse = 1.0 / (1.0 + lower + upper + lower * ratio_before)
        ratio = -upper * inverse
        out_ref[k, INV : INV + 16] = inverse
        out_ref[k, RATIO : RATIO + 16] = ratio
        out_ref[k, LOWER : LOWER + 16] = lower
        return ratio, upper

    zero = jnp.zeros((16, LANES), jnp.float32)
    lax.fori_loop(0, NZ, level, (zero, zero))


def edge(outer_lo, inner_lo, inner_hi, outer_hi):
    value = 7.0 / 12.0 * (inner_lo + inner_hi) - 1.0 / 12.0 * (outer_lo + outer_hi)
    return jnp.minimum(
        jnp.maximum(value, jnp.minimum(inner_lo, inner_hi)), jnp.maximum(inner_lo, inner_hi)
    )


def face(courant, half, slope, low_edge, near, high_edge, low_cell, high_cell):
    positive = courant > 0
    far = jnp.where(positive, low_edge, high_edge)
    cell = jnp.where(positive, low_cell, high_cell)
    curve = 6.0 * cell - 3.0 * (near + far)
    return courant * (near - half * ((near - far) - slope * curve))


def ahead(value, count):
    return pltpu.roll(value, (LANES - count) % LANES, 1)


def along_y(q, courant, half, slope):
    q_next = ahead(q, 1)
    edges = edge(pltpu.roll(q, 1, 1), q, q_next, ahead(q, 2))
    return face(
        courant, half, slope, pltpu.roll(edges, 1, 1), edges, ahead(edges, 1), q, q_next
    )


def step_kernel(low_row, high_row, base, last, q_ref, coef_ref, east_ref, west_ref,
                from_west_ref, from_east_ref, rates_ref, *refs):
    if last:
        ends_ref, out_ref, forward_ref, flux_ref = refs
    else:
        out_ref, pack_east_ref, pack_west_ref, *message_refs, ends_ref, forward_ref, flux_ref = refs
    rows = list(range(low_row, high_row))
    rates = spun(rates_ref)
    lane = lax.broadcasted_iota(jnp.int32, (TR, LANES), 1)
    place = lane % 8

    def coef(k, at, row):
        return jnp.broadcast_to(coef_ref[k, pl.ds(at + spot(row), 1), :], (TR, LANES))

    def end_faces(k, from_west, from_east):
        low = jnp.broadcast_to(coef_ref[k, pl.ds(ENDS, 1), :], (TR, LANES))
        high = jnp.broadcast_to(coef_ref[k, pl.ds(ENDS + 1, 1), :], (TR, LANES))
        low = jnp.where(place == 2, low * pltpu.roll(from_west, LANES - 1, 1), low)
        high = jnp.where(place == 4, high * from_east, high)
        ends_ref[k, 0], ends_ref[k, 1] = low, high
        return low, high

    def strip(courant, value):
        size = jnp.abs(courant)
        return along_y(value, courant, 0.5 * size, 1.0 - size * (2.0 / 3.0))

    forward_ref[...] = jnp.zeros_like(forward_ref)
    flux_ref[...] = jnp.zeros_like(flux_ref)

    def down(k):
        below = jnp.minimum(k + 1, NZ - 1)
        from_west = received(from_west_ref, k, True)
        from_east = received(from_east_ref, k, False)
        if last:
            low, high = ends_ref[k, 0], ends_ref[k, 1]
        else:
            low, high = end_faces(k, from_west, from_east)
        strip_w = strip(low, jnp.where(place < 3, from_west, east_ref[k]))
        strip_e = strip(high, jnp.where(place < 5, west_ref[k], from_east))
        edges, flux_x = {}, {}

        def q(row):
            return q_ref[k, row + base]

        def edge_at(row):
            if row not in edges:
                edges[row] = edge(q(row - 1), q(row), q(row + 1), q(row + 2))
            return edges[row]

        def flux_at(row):
            if row not in flux_x:
                flux_x[row] = face(
                    coef(k, UX, row), coef(k, AX, row), coef(k, BX, row),
                    edge_at(row - 1), edge_at(row), edge_at(row + 1), q(row), q(row + 1),
                )
            return flux_x[row]

        for index, row in enumerate(rows):
            here = q(row)
            flux_y = along_y(here, coef(k, UY, row), coef(k, AY, row), coef(k, BY, row))
            at = 8 * (row + 3)
            low_end = pltpu.roll(strip_w, (LANES - at - 3) % LANES, 1)
            high_end = pltpu.roll(strip_e, (123 - at) % LANES, 1)
            flux_y = jnp.where(lane < 2, low_end, jnp.where(lane >= 125, high_end, flux_y))
            flux_south = pltpu.roll(jnp.where(lane == 127, low_end, flux_y), 1, 1)
            courant_z = coef(k, CZ, row)
            flux_z = courant_z * jnp.where(courant_z > 0, here, q_ref[below, row + base])
            advected = here - (
                (flux_at(row) - flux_at(row - 1)) + (flux_y - flux_south)
                + (flux_z - flux_ref[index])
            )
            flux_ref[index] = flux_z
            forward_ref[k + 1, index] = (
                advected + coef(k, LOWER, row) * forward_ref[k, index]
            ) * coef(k, INV, row)

    @pl.loop(0, NZ // UNROLL)
    def _(part):
        for index in range(UNROLL):
            down(part * UNROLL + index)

    flux_ref[...] = jnp.zeros_like(flux_ref)

    def up(k):
        own = {}
        for index, row in enumerate(rows):
            value = forward_ref[k + 1, index] - coef(k, RATIO, row) * flux_ref[index]
            flux_ref[index] = value
            if last:
                out_ref[pl.ds(k * 8 + row, TR, stride=NZ * 8), :] = value
            else:
                value = react(value, rates)
                out_ref[k, index] = value
                if 0 <= row < 8:
                    own[row] = value
        if not last:
            east, west = pack(own.values(), own.keys())
            pack_east_ref[k], pack_west_ref[k] = east, west
            merge(message_refs[0], k, east, True)
            merge(message_refs[1], k, west, False)

    @pl.loop(0, NZ // UNROLL)
    def _(part):
        for index in range(UNROLL):
            up(NZ - 1 - part * UNROLL - index)


def transport(tracers, reaction, velocity, thickness, sea_mask, bottom, diffusivity):
    groups, stripes, count = lax.axis_size("dy"), lax.axis_size("dx") // XS, lax.axis_size("dx")
    group = lax.axis_index("group").astype(jnp.int32).reshape(1)
    x_index = (lax.axis_index("dx") % XS).astype(jnp.int32).reshape(1)

    def dx_pairs(forth, back):
        pairs = []
        for stripe in range(stripes):
            for source, target, far in forth:
                if 0 <= stripe + far < stripes and (far or stripe + 1 < stripes):
                    pairs.append((stripe * XS + source, (stripe + far) * XS + target))
            for source, target, far in back:
                if 0 <= stripe - far < stripes and (far or stripe > 0):
                    pairs.append((stripe * XS + source, (stripe - far) * XS + target))
        return pairs

    def collect_pairs(forth, back):
        pairs = []
        for stripe in range(stripes):
            if stripe > 0:
                pairs += [(stripe * XS + s, stripe * XS + t) for s, t in forth]
            if stripe + 1 < stripes:
                pairs += [(stripe * XS + s, stripe * XS + t) for s, t in back]
        return pairs

    sizes = [n for _, n in PIECES.values()]
    hi, lo, *far = call(
        first_kernel,
        [shape_of(NZ, HALO, TR, LANES)] * 2 + [shape_of(n, HALO, TR, LANES) for n in sizes],
        [x_index], [], (), [tracers.reshape(-1, LANES), sea_mask, bottom, reaction],
    )
    velocity, thickness, sea_mask, bottom, diffusivity, far = lax.optimization_barrier(
        (velocity, thickness, sea_mask, bottom, diffusivity, far)
    )
    far = dict(zip(PIECES, far))
    far["A"] = lax.ppermute(far["A"], "dx", dx_pairs([(3, 2, 0)], [(0, 1, 0)]))
    far["B"] = lax.ppermute(far["B"], "dx", dx_pairs([(3, 0, 0)], [(0, 3, 0)]))
    far["C"] = lax.ppermute(far["C"], "dx", dx_pairs([(3, 1, 0)], [(0, 2, 0)]))
    far["O"] = lax.ppermute(far["O"], "dx", dx_pairs([(3, 3, 1)], [(0, 0, 1)]))
    far["A"] = lax.ppermute(far["A"], "dx", dx_pairs([(2, 2, 1)], [(1, 1, 1)]))
    far["B"] = lax.ppermute(far["B"], "dx", dx_pairs([(0, 0, 1)], [(3, 3, 1)]))
    far["C"] = lax.ppermute(far["C"], "dx", dx_pairs([(1, 1, 1)], [(2, 2, 1)]))
    inside = [(i, i + 1) for i in range(count - 1) if i % XS != XS - 1]
    outside = [(b, a) for a, b in inside]
    from_west = lax.ppermute(hi, "dx", inside)
    from_east = lax.ppermute(lo, "dx", outside)
    far["O"] = lax.ppermute(far["O"], "dx", collect_pairs([(3, 0)], [(0, 3)]))
    far["A"] = lax.ppermute(far["A"], "dx", collect_pairs([(2, 0)], [(1, 3)]))
    far["C"] = lax.ppermute(far["C"], "dx", collect_pairs([(1, 0)], [(2, 3)]))

    levels = thickness.shape[0]
    items = 4 * levels + 1
    slab = 0.3 * jnp.tanh(velocity) * thickness[None]
    rim = shape_of((items + 1) // 2, 8, LANES)

    own, rim_low, rim_high, rim_far = call(
        own_kernel, [shape_of(items, 8, LANES)] + [rim] * 3, [group, x_index], [slab], (),
        [sea_mask, bottom, diffusivity],
    )
    rim_west = lax.ppermute(rim_high, "dx", inside)
    rim_east = lax.ppermute(rim_low, "dx", outside)
    swapped = [(i, i + 1) for i in range(count - 1) if i % XS == XS - 1]
    rim_far = lax.ppermute(rim_far, "dx", swapped + [(b, a) for a, b in swapped])
    north = [(i, i + 1) for i in range(groups - 1)]
    south = [(b, a) for a, b in north]
    (table,) = call(
        table_kernel, [shape_of(levels, 72, LANES)], [group, x_index],
        [own, rim_west, rim_east, rim_far],
        [pltpu.VMEM((items, 16, LANES), jnp.float32), pltpu.VMEM((16, LANES), jnp.float32)],
    )
    members = lax.axis_size("group")

    def gather(value, flip, turn):
        pairs = [((i + 2 * turn) % members ^ flip, i) for i in range(members)]
        return lax.ppermute(value, "group", pairs)

    turns = [1, 3, 2] if members == 8 else list(range(1, members // 2))
    along = [table] + [gather(table, 0, turn) for turn in turns]
    across = [gather(value, 1, 0) for value in along]
    order = [(flip, turn) for flip in (0, 1) for turn in [0] + turns]
    (coefs,) = call(
        functools.partial(coefficient_kernel, order), [shape_of(NZ, ENDS + 8, LANES)],
        [group], along + across,
    )

    def swap(east, west):
        return lax.ppermute(east, "dy", north), lax.ppermute(west, "dy", south)

    packs = [shape_of(NZ, TR, LANES)] * 2
    messages = [shape_of(HALF, TR, LANES)] * 2
    own_ends = call(ends_kernel, packs, [], [hi, lo])
    joined, east, west, *sent = call(
        join_kernel, [shape_of(NZ, 20, TR, LANES)] + packs + messages, [x_index],
        [hi, lo, from_west, from_east] + [far[name] for name in PIECES] + [coefs, *own_ends],
    )

    def scratch(rows):
        return [
            pltpu.VMEM((NZ + 1, rows, TR, LANES), jnp.float32),
            pltpu.VMEM((rows, TR, LANES), jnp.float32),
        ]

    middle, east2, west2, *sent2, ends = call(
        functools.partial(step_kernel, -3, 11, HALO, False),
        [shape_of(NZ, 14, TR, LANES)] + packs + messages + [shape_of(NZ, 2, TR, LANES)],
        [],
        [joined, coefs, east, west, *swap(*sent), reaction], scratch(14),
    )
    (out,) = call(
        functools.partial(step_kernel, 0, 8, 3, True),
        [jax.ShapeDtypeStruct((TR * NZ * 8, LANES), jnp.float32)], [],
        [middle, coefs, east2, west2, *swap(*sent2), reaction, ends], scratch(8),
    )
    return out.reshape(TR, NZ, 8, LANES)


def solution(mesh):
    placed = (
        P("group", None, "dx", "dy"),
        P("group", None),
        P(None, "group", "dx", "dy"),
        P("group", "dx", "dy"),
        P("dx", "dy"),
        P("dx", "dy"),
        P(None, "dx", "dy"),
    )
    return jax.shard_map(
        transport,
        mesh=mesh,
        in_specs=placed,
        out_specs=P("group", None, "dx", "dy"),
        check_vma=False,
    )
```

```python
import functools

import jax
import jax.numpy as jnp
from jax import lax
from jax.experimental import pallas as pl
from jax.experimental.pallas import tpu as pltpu
from jax.sharding import PartitionSpec as P

INTERPRET = False
XS = 4
NZ = 32
TR = 8
LANES = 128
HALO = 6
VMEM_LIMIT = 24 << 20
UNROLL = 2
PIECES = {"O": (0, 5), "A": (5, 12), "B": (17, 8), "C": (25, 7)}


def spot(row):
    if row < 0:
        return 12 + row
    return row if row < 8 else row + 4


def vmem(count):
    return [pl.BlockSpec(memory_space=pltpu.VMEM)] * count


def shape_of(*dims):
    if INTERPRET:
        return jax.ShapeDtypeStruct(dims, jnp.float32)
    return pltpu.VMEM(dims, jnp.float32)


def stored(value):
    return value if INTERPRET else pltpu.with_memory_space_constraint(value, pltpu.HBM)


def kept(value):
    return value if INTERPRET else pltpu.with_memory_space_constraint(value, pltpu.VMEM)


def fetched(body, skip, count):
    def wrapped(*refs):
        *refs, arrivals = refs
        sources, places = refs[skip : skip + count], refs[len(refs) - count :]
        copies = [
            pltpu.make_async_copy(source, place, arrivals.at[index])
            for index, (source, place) in enumerate(zip(sources, places))
        ]
        for copy in copies:
            copy.start()
        for copy in copies:
            copy.wait()
        body(*refs[:skip], *places, *refs[skip + count : len(refs) - count])

    return wrapped if count else body


def call(body, outs, scalars, arrays, scratch=(), arguments=()):
    return pl.pallas_call(
        fetched(body, len(scalars), len(arguments)),
        out_shape=outs,
        in_specs=[pl.BlockSpec(memory_space=pltpu.SMEM)] * len(scalars)
        + [pl.BlockSpec(memory_space=pltpu.HBM)] * len(arguments)
        + vmem(len(arrays)),
        out_specs=vmem(len(outs)),
        scratch_shapes=list(scratch)
        + [pltpu.VMEM(value.shape, value.dtype) for value in arguments]
        + [pltpu.SemaphoreType.DMA((len(arguments),))] * bool(arguments),
        compiler_params=pltpu.CompilerParams(vmem_limit_bytes=VMEM_LIMIT),
        interpret=INTERPRET,
    )(*scalars, *map(stored, arguments), *map(kept, arrays))


def spun(rates_ref):
    rates = rates_ref[...]
    tracer = lax.broadcasted_iota(jnp.int32, (TR, TR), 0)
    other = lax.broadcasted_iota(jnp.int32, (TR, TR), 1)
    spins = []
    for shift in range(TR):
        picked = jnp.where(other == (tracer + TR - shift) % TR, rates, 0.0)
        spins.append(jnp.broadcast_to(jnp.sum(picked, axis=1, keepdims=True), (TR, LANES)))
    return spins


def react(value, rates):
    total = rates[0] * value
    for shift in range(1, TR):
        total = total + rates[shift] * pltpu.roll(value, shift, 0)
    return value + value * total


def first_kernel(x_ref, tracers_ref, sea_ref, bottom_ref, rates_ref, hi_ref, lo_ref, *far_refs):
    depth = sea_ref[...] * bottom_ref[...]
    depths = [jnp.broadcast_to(depth[row : row + 1], (TR, LANES)) for row in range(8)]
    rates = spun(rates_ref)

    def level(k, carry):
        for row in range(8):
            value = tracers_ref[pl.ds(k * 8 + row, TR, stride=NZ * 8), :]
            value = react(jnp.where(k < depths[row], value, 0.0), rates)
            if row < HALO:
                lo_ref[k, row] = value
            if row >= 8 - HALO:
                hi_ref[k, row - (8 - HALO)] = value
        return carry

    lax.fori_loop(0, NZ, level, 0)
    for far_ref, (first, count) in zip(far_refs, PIECES.values()):

        @pl.when(x_ref[0] == XS - 1)
        def _():
            far_ref[...] = hi_ref[first : first + count]

        @pl.when(x_ref[0] != XS - 1)
        def _():
            far_ref[...] = lo_ref[first : first + count]


def pack(values, rows, east=None, west=None):
    lane = lax.broadcasted_iota(jnp.int32, (TR, LANES), 1)
    slot = lane // 8
    if east is None:
        east = west = jnp.zeros((TR, LANES), jnp.float32)
    for value, row in zip(values, rows):
        place = 8 * (row + 3)
        here = slot == row + 3
        east = jnp.where(here, pltpu.roll(value, (place + 3) % LANES, 1), east)
        west = jnp.where(here, pltpu.roll(value, (place + 5) % LANES, 1), west)
    return east, west


def ends_kernel(hi_ref, lo_ref, east_ref, west_ref):
    def level(k, carry):
        values = [lo_ref[k, row] for row in range(HALO)]
        values += [hi_ref[k, row] for row in range(2 * HALO - 8, HALO)]
        east_ref[k], west_ref[k] = pack(values, range(8))
        return carry

    lax.fori_loop(0, NZ, level, 0)


def join_kernel(x_ref, hi_ref, lo_ref, west_ref, east_ref, *refs):
    pieces, (coef_ref, own_east_ref, own_west_ref, all_ref, *pack_refs) = refs[:4], refs[4:]
    pack_east_ref, pack_west_ref, send_east_ref, send_west_ref = pack_refs
    place = lax.broadcasted_iota(jnp.int32, (TR, LANES), 1) % 8
    for near_ref, owner, base in ((west_ref, 0, 0), (east_ref, XS - 1, HALO + 8)):

        @pl.when(x_ref[0] == owner)
        def _():
            for piece_ref, (first, count) in zip(pieces, PIECES.values()):
                all_ref[first : first + count, base : base + HALO] = piece_ref[...]

        @pl.when(x_ref[0] != owner)
        def _():
            all_ref[:, base : base + HALO] = near_ref[...]

    all_ref[:, HALO : 2 * HALO] = lo_ref[...]
    all_ref[:, 2 * HALO : 2 * HALO + 2] = hi_ref[:, HALO - 2 : HALO]
    rows = [-3, -2, -1, 8, 9, 10]

    def level(k, carry):
        east, west = pack(
            [all_ref[k, row + HALO] for row in rows], rows, own_east_ref[k], own_west_ref[k]
        )
        pack_east_ref[k], pack_west_ref[k] = east, west
        last_face = jnp.broadcast_to(coef_ref[k, pl.ds(ENDS + 1, 1)], (TR, LANES))
        first_wet = jnp.broadcast_to(coef_ref[k, pl.ds(ENDS, 1)], (TR, LANES))
        last_face = pltpu.roll(last_face, LANES - 1, 1)
        first_wet = pltpu.roll(first_wet, 2, 1)
        send_east_ref[k] = jnp.where(place < 3, east, last_face)
        send_west_ref[k] = jnp.where(place < 5, first_wet, west)
        return carry

    lax.fori_loop(0, NZ, level, 0)


UX, AX, BX, UY, AY, BY, CZ, INV, RATIO, LOWER = range(0, 160, 16)
ENDS = 160


def own_kernel(group_ref, x_ref, sea_ref, bottom_ref, mix_ref, slab_ref, own_ref, *rim_refs):
    levels = slab_ref.shape[1]
    first_level = group_ref[0] * levels
    for kind in range(3):
        own_ref[kind * levels : (kind + 1) * levels] = slab_ref[kind]
    own_ref[3 * levels : 4 * levels] = mix_ref[pl.ds(first_level, levels)]
    own_ref[4 * levels] = (sea_ref[...] * bottom_ref[...]).astype(jnp.float32)
    low_ref, high_ref, far_ref = rim_refs
    low_ref[...] = jnp.zeros_like(low_ref)
    high_ref[...] = jnp.zeros_like(high_ref)
    for item in range(own_ref.shape[0]):
        place = pl.ds(4 * (item % 2), 4)
        low_ref[item // 2, place] = own_ref[item, 0:4]
        high_ref[item // 2, place] = own_ref[item, 4:8]
    far_ref[...] = jnp.where(x_ref[0] == XS - 1, high_ref[...], low_ref[...])


def table_kernel(group_ref, x_ref, own_ref, west_ref, east_ref, far_ref, table_ref, blocks_ref,
                 next_ref):
    items = own_ref.shape[0]
    levels = items // 4
    blocks_ref[:, 0:8] = own_ref[...]
    for item in range(items):
        place = pl.ds(4 * (item % 2), 4)
        far = far_ref[item // 2, place]
        blocks_ref[item, 8:12] = jnp.where(x_ref[0] == 0, far, west_ref[item // 2, place])
        blocks_ref[item, 12:16] = jnp.where(x_ref[0] == XS - 1, far, east_ref[item // 2, place])
    lane = lax.broadcasted_iota(jnp.int32, (16, LANES), 1)
    slot = lax.broadcasted_iota(jnp.int32, (8, LANES), 1) // 8
    depth = blocks_ref[items - 1]
    for target, source, count in ((0, 1, 7), (7, 12, 1), (8, 9, 3), (11, 0, 1), (12, 13, 3)):
        next_ref[target : target + count] = blocks_ref[items - 1, source : source + count]
    next_ref[15:16] = jnp.zeros((1, LANES), jnp.float32)
    depth_x = jnp.minimum(depth, next_ref[...])
    depth_y = jnp.where(
        lane == LANES - 1, depth, jnp.minimum(depth, pltpu.roll(depth, LANES - 1, 1))
    )
    depth_first = jnp.broadcast_to(depth[:, 0:1], (16, LANES))
    table_ref[...] = jnp.zeros_like(table_ref)
    for index in range(levels):
        level = (group_ref[0] * levels + index).astype(jnp.float32)
        courant_y = jnp.where(level < depth_y, blocks_ref[levels + index], 0.0)
        table_ref[index, 0:16] = jnp.where(level < depth_x, blocks_ref[index], 0.0)
        table_ref[index, 16:32] = courant_y
        wet_below = level + 1.0 < depth
        table_ref[index, 32:48] = jnp.where(wet_below, blocks_ref[2 * levels + index], 0.0)
        table_ref[index, 48:64] = jnp.where(wet_below, blocks_ref[3 * levels + index], 0.0)
        wet_first = jnp.where(level < depth_first, 1.0, 0.0)
        next_ref[...] = jnp.where(lane == LANES - 1, wet_first, courant_y)
        low = high = jnp.zeros((8, LANES), jnp.float32)
        for row in range(-3, 11):
            at = 8 * (row + 3)
            here = slot == row + 3
            place = pl.ds(spot(row), 1)
            low_row = jnp.broadcast_to(next_ref[place], (8, LANES))
            high_row = jnp.broadcast_to(table_ref[index, pl.ds(16 + spot(row), 1)], (8, LANES))
            low = jnp.where(here, pltpu.roll(low_row, (at + 3) % LANES, 1), low)
            high = jnp.where(here, pltpu.roll(high_row, (at + 5) % LANES, 1), high)
        table_ref[index, 64:65] = low[0:1]
        table_ref[index, 65:66] = high[0:1]


def coefficient_kernel(order, group_ref, *refs):
    pieces, out_ref = refs[:-1], refs[-1]
    levels = pieces[0].shape[0]
    for (flip, turn), piece_ref in zip(order, pieces):
        owner = (group_ref[0] // 2 + turn) % (len(order) // 2) * 2 + (group_ref[0] % 2 + flip) % 2

        def spread(index, carry):
            k = owner * levels + index
            for source, at in ((0, UX), (16, UY)):
                courant = piece_ref[index, source : source + 16]
                size = jnp.abs(courant)
                out_ref[k, at : at + 16] = courant
                out_ref[k, at + 16 : at + 32] = 0.5 * size
                out_ref[k, at + 32 : at + 48] = 1.0 - size * (2.0 / 3.0)
            out_ref[k, CZ : CZ + 16] = piece_ref[index, 32:48]
            out_ref[k, INV : INV + 16] = piece_ref[index, 48:64]
            out_ref[k, ENDS : ENDS + 8] = piece_ref[index, 64:72]
            return carry

        lax.fori_loop(0, levels, spread, 0)

    def level(k, carry):
        ratio_before, lower = carry
        upper = out_ref[k, INV : INV + 16]
        inverse = 1.0 / (1.0 + lower + upper + lower * ratio_before)
        ratio = -upper * inverse
        out_ref[k, INV : INV + 16] = inverse
        out_ref[k, RATIO : RATIO + 16] = ratio
        out_ref[k, LOWER : LOWER + 16] = lower
        return ratio, upper

    zero = jnp.zeros((16, LANES), jnp.float32)
    lax.fori_loop(0, NZ, level, (zero, zero))


def edge(outer_lo, inner_lo, inner_hi, outer_hi):
    value = 7.0 / 12.0 * (inner_lo + inner_hi) - 1.0 / 12.0 * (outer_lo + outer_hi)
    return jnp.minimum(
        jnp.maximum(value, jnp.minimum(inner_lo, inner_hi)), jnp.maximum(inner_lo, inner_hi)
    )


def face(courant, half, slope, low_edge, near, high_edge, low_cell, high_cell):
    positive = courant > 0
    far = jnp.where(positive, low_edge, high_edge)
    cell = jnp.where(positive, low_cell, high_cell)
    curve = 6.0 * cell - 3.0 * (near + far)
    return courant * (near - half * ((near - far) - slope * curve))


def ahead(value, count):
    return pltpu.roll(value, (LANES - count) % LANES, 1)


def along_y(q, courant, half, slope):
    q_next = ahead(q, 1)
    edges = edge(pltpu.roll(q, 1, 1), q, q_next, ahead(q, 2))
    return face(
        courant, half, slope, pltpu.roll(edges, 1, 1), edges, ahead(edges, 1), q, q_next
    )


def step_kernel(low_row, high_row, base, last, q_ref, coef_ref, east_ref, west_ref,
                from_west_ref, from_east_ref, rates_ref, *refs):
    if last:
        ends_ref, out_ref, forward_ref, flux_ref = refs
    else:
        out_ref, pack_east_ref, pack_west_ref, ends_ref, forward_ref, flux_ref = refs
    rows = list(range(low_row, high_row))
    rates = spun(rates_ref)
    lane = lax.broadcasted_iota(jnp.int32, (TR, LANES), 1)
    place = lane % 8

    def coef(k, at, row):
        return jnp.broadcast_to(coef_ref[k, pl.ds(at + spot(row), 1), :], (TR, LANES))

    def end_faces(k, from_west, from_east):
        low = jnp.broadcast_to(coef_ref[k, pl.ds(ENDS, 1), :], (TR, LANES))
        high = jnp.broadcast_to(coef_ref[k, pl.ds(ENDS + 1, 1), :], (TR, LANES))
        low = jnp.where(place == 2, low * pltpu.roll(from_west, LANES - 1, 1), low)
        high = jnp.where(place == 4, high * from_east, high)
        ends_ref[k, 0], ends_ref[k, 1] = low, high
        return low, high

    def strip(courant, value):
        size = jnp.abs(courant)
        return along_y(value, courant, 0.5 * size, 1.0 - size * (2.0 / 3.0))

    forward_ref[...] = jnp.zeros_like(forward_ref)
    flux_ref[...] = jnp.zeros_like(flux_ref)

    def down(k):
        below = jnp.minimum(k + 1, NZ - 1)
        from_west, from_east = from_west_ref[k], from_east_ref[k]
        if last:
            low, high = ends_ref[k, 0], ends_ref[k, 1]
        else:
            low, high = end_faces(k, from_west, from_east)
        strip_w = strip(low, jnp.where(place < 3, from_west, east_ref[k]))
        strip_e = strip(high, jnp.where(place < 5, west_ref[k], from_east))
        edges, flux_x = {}, {}

        def q(row):
            return q_ref[k, row + base]

        def edge_at(row):
            if row not in edges:
                edges[row] = edge(q(row - 1), q(row), q(row + 1), q(row + 2))
            return edges[row]

        def flux_at(row):
            if row not in flux_x:
                flux_x[row] = face(
                    coef(k, UX, row), coef(k, AX, row), coef(k, BX, row),
                    edge_at(row - 1), edge_at(row), edge_at(row + 1), q(row), q(row + 1),
                )
            return flux_x[row]

        for index, row in enumerate(rows):
            here = q(row)
            flux_y = along_y(here, coef(k, UY, row), coef(k, AY, row), coef(k, BY, row))
            at = 8 * (row + 3)
            low_end = pltpu.roll(strip_w, (LANES - at - 3) % LANES, 1)
            high_end = pltpu.roll(strip_e, (123 - at) % LANES, 1)
            flux_y = jnp.where(lane < 2, low_end, jnp.where(lane >= 125, high_end, flux_y))
            flux_south = pltpu.roll(jnp.where(lane == 127, low_end, flux_y), 1, 1)
            courant_z = coef(k, CZ, row)
            flux_z = courant_z * jnp.where(courant_z > 0, here, q_ref[below, row + base])
            advected = here - (
                (flux_at(row) - flux_at(row - 1)) + (flux_y - flux_south)
                + (flux_z - flux_ref[index])
            )
            flux_ref[index] = flux_z
            forward_ref[k + 1, index] = (
                advected + coef(k, LOWER, row) * forward_ref[k, index]
            ) * coef(k, INV, row)

    @pl.loop(0, NZ // UNROLL)
    def _(part):
        for index in range(UNROLL):
            down(part * UNROLL + index)

    flux_ref[...] = jnp.zeros_like(flux_ref)

    def up(k):
        own = {}
        for index, row in enumerate(rows):
            value = forward_ref[k + 1, index] - coef(k, RATIO, row) * flux_ref[index]
            flux_ref[index] = value
            if last:
                out_ref[pl.ds(k * 8 + row, TR, stride=NZ * 8), :] = value
            else:
                value = react(value, rates)
                out_ref[k, index] = value
                if 0 <= row < 8:
                    own[row] = value
        if not last:
            pack_east_ref[k], pack_west_ref[k] = pack(own.values(), own.keys())

    @pl.loop(0, NZ // UNROLL)
    def _(part):
        for index in range(UNROLL):
            up(NZ - 1 - part * UNROLL - index)


def transport(tracers, reaction, velocity, thickness, sea_mask, bottom, diffusivity):
    groups, stripes, count = lax.axis_size("dy"), lax.axis_size("dx") // XS, lax.axis_size("dx")
    group = lax.axis_index("group").astype(jnp.int32).reshape(1)
    x_index = (lax.axis_index("dx") % XS).astype(jnp.int32).reshape(1)

    def dx_pairs(forth, back):
        pairs = []
        for stripe in range(stripes):
            for source, target, far in forth:
                if 0 <= stripe + far < stripes and (far or stripe + 1 < stripes):
                    pairs.append((stripe * XS + source, (stripe + far) * XS + target))
            for source, target, far in back:
                if 0 <= stripe - far < stripes and (far or stripe > 0):
                    pairs.append((stripe * XS + source, (stripe - far) * XS + target))
        return pairs

    def collect_pairs(forth, back):
        pairs = []
        for stripe in range(stripes):
            if stripe > 0:
                pairs += [(stripe * XS + s, stripe * XS + t) for s, t in forth]
            if stripe + 1 < stripes:
                pairs += [(stripe * XS + s, stripe * XS + t) for s, t in back]
        return pairs

    sizes = [n for _, n in PIECES.values()]
    hi, lo, *far = call(
        first_kernel,
        [shape_of(NZ, HALO, TR, LANES)] * 2 + [shape_of(n, HALO, TR, LANES) for n in sizes],
        [x_index], [], (), [tracers.reshape(-1, LANES), sea_mask, bottom, reaction],
    )
    velocity, thickness, sea_mask, bottom, diffusivity, far = lax.optimization_barrier(
        (velocity, thickness, sea_mask, bottom, diffusivity, far)
    )
    far = dict(zip(PIECES, far))
    far["A"] = lax.ppermute(far["A"], "dx", dx_pairs([(3, 2, 0)], [(0, 1, 0)]))
    far["B"] = lax.ppermute(far["B"], "dx", dx_pairs([(3, 0, 0)], [(0, 3, 0)]))
    far["C"] = lax.ppermute(far["C"], "dx", dx_pairs([(3, 1, 0)], [(0, 2, 0)]))
    far["O"] = lax.ppermute(far["O"], "dx", dx_pairs([(3, 3, 1)], [(0, 0, 1)]))
    far["A"] = lax.ppermute(far["A"], "dx", dx_pairs([(2, 2, 1)], [(1, 1, 1)]))
    far["B"] = lax.ppermute(far["B"], "dx", dx_pairs([(0, 0, 1)], [(3, 3, 1)]))
    far["C"] = lax.ppermute(far["C"], "dx", dx_pairs([(1, 1, 1)], [(2, 2, 1)]))
    inside = [(i, i + 1) for i in range(count - 1) if i % XS != XS - 1]
    outside = [(b, a) for a, b in inside]
    from_west = lax.ppermute(hi, "dx", inside)
    from_east = lax.ppermute(lo, "dx", outside)
    far["O"] = lax.ppermute(far["O"], "dx", collect_pairs([(3, 0)], [(0, 3)]))
    far["A"] = lax.ppermute(far["A"], "dx", collect_pairs([(2, 0)], [(1, 3)]))
    far["C"] = lax.ppermute(far["C"], "dx", collect_pairs([(1, 0)], [(2, 3)]))

    levels = thickness.shape[0]
    items = 4 * levels + 1
    slab = 0.3 * jnp.tanh(velocity) * thickness[None]
    rim = shape_of((items + 1) // 2, 8, LANES)

    own, rim_low, rim_high, rim_far = call(
        own_kernel, [shape_of(items, 8, LANES)] + [rim] * 3, [group, x_index], [slab], (),
        [sea_mask, bottom, diffusivity],
    )
    rim_west = lax.ppermute(rim_high, "dx", inside)
    rim_east = lax.ppermute(rim_low, "dx", outside)
    swapped = [(i, i + 1) for i in range(count - 1) if i % XS == XS - 1]
    rim_far = lax.ppermute(rim_far, "dx", swapped + [(b, a) for a, b in swapped])
    north = [(i, i + 1) for i in range(groups - 1)]
    south = [(b, a) for a, b in north]
    (table,) = call(
        table_kernel, [shape_of(levels, 72, LANES)], [group, x_index],
        [own, rim_west, rim_east, rim_far],
        [pltpu.VMEM((items, 16, LANES), jnp.float32), pltpu.VMEM((16, LANES), jnp.float32)],
    )
    members = lax.axis_size("group")

    def gather(value, flip, turn):
        pairs = [((i + 2 * turn) % members ^ flip, i) for i in range(members)]
        return lax.ppermute(value, "group", pairs)

    turns = [1, 3, 2] if members == 8 else list(range(1, members // 2))
    along = [table] + [gather(table, 0, turn) for turn in turns]
    across = [gather(value, 1, 0) for value in along]
    order = [(flip, turn) for flip in (0, 1) for turn in [0] + turns]
    (coefs,) = call(
        functools.partial(coefficient_kernel, order), [shape_of(NZ, ENDS + 8, LANES)],
        [group], along + across,
    )

    def swap(east, west):
        return lax.ppermute(east, "dy", north), lax.ppermute(west, "dy", south)

    packs = [shape_of(NZ, TR, LANES)] * 2
    own_ends = call(ends_kernel, packs, [], [hi, lo])
    joined, east, west, *sent = call(
        join_kernel, [shape_of(NZ, 20, TR, LANES)] + packs * 2, [x_index],
        [hi, lo, from_west, from_east] + [far[name] for name in PIECES] + [coefs, *own_ends],
    )

    def scratch(rows):
        return [
            pltpu.VMEM((NZ + 1, rows, TR, LANES), jnp.float32),
            pltpu.VMEM((rows, TR, LANES), jnp.float32),
        ]

    middle, east2, west2, ends = call(
        functools.partial(step_kernel, -3, 11, HALO, False),
        [shape_of(NZ, 14, TR, LANES)] + packs + [shape_of(NZ, 2, TR, LANES)], [],
        [joined, coefs, east, west, *swap(*sent), reaction], scratch(14),
    )
    (out,) = call(
        functools.partial(step_kernel, 0, 8, 3, True),
        [jax.ShapeDtypeStruct((TR * NZ * 8, LANES), jnp.float32)], [],
        [middle, coefs, east2, west2, *swap(east2, west2), reaction, ends], scratch(8),
    )
    return out.reshape(TR, NZ, 8, LANES)


def solution(mesh):
    placed = (
        P("group", None, "dx", "dy"),
        P("group", None),
        P(None, "group", "dx", "dy"),
        P("group", "dx", "dy"),
        P("dx", "dy"),
        P("dx", "dy"),
        P(None, "dx", "dy"),
    )
    return jax.shard_map(
        transport,
        mesh=mesh,
        in_specs=placed,
        out_specs=P("group", None, "dx", "dy"),
        check_vma=False,
    )
```
